256 devices in a mesh: tm: 8 (over x, core), tile: 32 (over y, z).
Axes of the slice: x: 4, y: 4, z: 8, core: 2. Of those that a mesh axis runs over, the one named last changes fastest.
Arguments:
- advect_east: float32 [8, 2, 384, 1440], P('tm', None, 'tile'), may hold values from -0.15 to 0.15
- advect_north: float32 [8, 2, 384, 1440], P('tm', None, 'tile'), may hold values from -0.15 to 0.15
- diffusion: float32 [8, 2, 384, 1440], P('tm', None, 'tile'), may hold values from 0.06 to 0.22
- background_var: float32 [8, 4, 2, 384, 1440], P('tm', None, None, 'tile'), may hold values from 0.3 to 3
- obs_cell: int32 [8, 32, 1024], P('tm', 'tile'), may hold values from 0 to 138239
- obs_value: float32 [8, 32, 1024], P('tm', 'tile'), may hold values from -6 to 6
- obs_weight: float32 [8, 32, 1024], P('tm', 'tile'), may hold values from 0.5 to 2
- obs_count: int32 [8, 32, 32], P('tm', 'tile'), may hold values from 10 to 32, as said below
Outputs:
- increment: float32 [8, 4, 2, 384, 1440], P('tm', None, None, 'tile')
The draws below stay inside these ranges and needn't reach their ends.
Inputs may be any that keep to these rules, and one draw needn't show every extreme that they name: In every sub-window one tile, drawn from the seed, gets 32 filled slots from every source device; only the first obs_count slots of a block hold observations.
All inputs are finite; a program needn't handle non-finite values.
Results may differ from the reference program's by a relative error of at most 0.00002.
Values sent between devices are 32-bit elements; how exact they have to be, the bound alone decides.
A program may use at most 128 MiB of HBM per device.

```python
import math
import jax
import jax.numpy as jnp
from jax import lax

VARS = 4
LEV = 2
LON = 1440
LAT_DEV = 12
CAP = 32
STEPS = 2
ITERS = 2
SUBS = 8
TILES = 32
NLAT = 384
ROWS = 96


def draw_obs_count(key, part):
    drawn = jax.random.randint(key, (SUBS, TILES, TILES), CAP // 3, CAP + 1, dtype=jnp.int32)
    crowded = jax.random.randint(jax.random.fold_in(key, 7), (SUBS, 1, 1), 0, TILES, dtype=jnp.int32)
    column = lax.broadcasted_iota(jnp.int32, (SUBS, TILES, TILES), 2)
    return jnp.where(column == crowded, CAP, drawn)


def touch_ends(entries, stream_key, least, largest):
    dims = entries.shape
    index_at = [jax.random.randint(jax.random.fold_in(stream_key, axis), (), 0, dims[axis]) for axis in range(len(dims))]
    entries = entries.at[tuple(index_at)].set(least)
    longest = dims.index(max(dims))
    index_at[longest] = (index_at[longest] + 1) % dims[longest]
    return entries.at[tuple(index_at)].set(largest)


def block_scale(key, extent, shards, low, high):
    def one(position, parts):
        steps = jax.random.uniform(jax.random.fold_in(jax.random.fold_in(key, 6), position), (parts,), jnp.float32, low / len(shards), high / len(shards))
        return jnp.repeat(jnp.exp(steps), extent[position] // parts).reshape((-1,) + (1,) * (len(extent) - position - 1))

    level = one(*shards[0])
    for cut in shards[1:]:
        level = level * one(*cut)
    return level


def gaussian(rng, extent, deviation, bound, pieces=(), kind=jnp.bfloat16):
    entries = jax.random.normal(rng, extent, jnp.float32) * deviation
    if len(pieces) > 0:
        entries = block_scale(rng, extent, pieces, -0.22, 0.18) * entries
    return jnp.clip(entries, min=-bound, max=bound).astype(kind)


def setup_inputs(seed: int = 0) -> dict:
    streams_of = jax.random.split(jax.random.key(seed), 9)
    advect_east = jnp.clip(jax.random.uniform(streams_of[0], (SUBS, LEV, NLAT, LON), jnp.float32, -0.15, 0.15) * block_scale(streams_of[0], (SUBS, LEV, NLAT, LON), ((0, 8), (2, 32)), -0.4, 0.0), -0.15, 0.15)
    advect_north = jnp.clip(jax.random.uniform(streams_of[1], (SUBS, LEV, NLAT, LON), jnp.float32, -0.15, 0.15) * block_scale(streams_of[1], (SUBS, LEV, NLAT, LON), ((0, 8), (2, 32)), -0.4, 0.0), -0.15, 0.15)
    diffusion = jnp.clip(0.06 + 0.16 * jax.random.uniform(streams_of[2], (SUBS, LEV, NLAT, LON), jnp.float32) ** block_scale(streams_of[2], (SUBS, LEV, NLAT, LON), ((0, 8), (2, 32)), -0.2, 0.2), 0.06, 0.22)
    background_var = jnp.clip(jnp.exp(math.log(3.0) - 2.3025851 * jax.random.uniform(streams_of[3], (SUBS, VARS, LEV, NLAT, LON), jnp.float32) ** block_scale(streams_of[3], (SUBS, VARS, LEV, NLAT, LON), ((0, 8), (3, 32)), -0.2, 0.2)), 0.3, 3.0)
    obs_cell = touch_ends(jax.random.randint(streams_of[4], (SUBS, TILES, TILES * CAP), 0, ROWS * LON), jax.random.fold_in(streams_of[4], 1), 0, (ROWS * LON) - 1).astype(jnp.int32)
    obs_value = gaussian(streams_of[5], (SUBS, TILES, TILES * CAP), 1.0, 6.0, ((0, 8), (1, 32)), jnp.float32)
    obs_weight = jnp.clip(jnp.exp(math.log(2.0) - 1.3862944 * jax.random.uniform(streams_of[6], (SUBS, TILES, TILES * CAP), jnp.float32) ** block_scale(streams_of[6], (SUBS, TILES, TILES * CAP), ((0, 8), (1, 32)), -0.2, 0.2)), 0.5, 2.0)
    obs_count = draw_obs_count(jax.random.fold_in(streams_of[8], 71), 0)
    return dict(advect_east=advect_east, advect_north=advect_north, diffusion=diffusion, background_var=background_var, obs_cell=obs_cell, obs_value=obs_value, obs_weight=obs_weight, obs_count=obs_count)


def model_step(field, east_c, north_c, diff_c):
    padded = jnp.pad(field, ((0, 0), (0, 0), (1, 1), (0, 0)))
    to_north = padded[:, :, 2:]
    to_south = padded[:, :, :-2]
    to_east = jnp.roll(field, -1, axis=-1)
    to_west = jnp.roll(field, 1, axis=-1)
    return (1.0 - 4.0 * diff_c) * field + (diff_c - 0.5 * east_c) * to_east + (diff_c + 0.5 * east_c) * to_west + (diff_c - 0.5 * north_c) * to_north + (diff_c + 0.5 * north_c) * to_south

def forward_map(forcing, advect_east, advect_north, diffusion):
    carried = jnp.zeros(forcing.shape[1:], jnp.float32)
    states = []
    for window in range(SUBS):
        carried = carried + forcing[window]
        for repeat in range(STEPS):
            carried = model_step(carried, advect_east[window], advect_north[window], diffusion[window])
        states.append(carried)
    return jnp.stack(states)

def reference(advect_east, advect_north, diffusion, background_var, obs_cell, obs_value, obs_weight, obs_count):
    shaped = (SUBS, TILES, TILES, CAP)
    cells = obs_cell.reshape(shaped)
    values = obs_value.reshape(shaped)
    weights = obs_weight.reshape(shaped)
    obs_row = cells // LON
    obs_lon = cells % LON
    variable = obs_row // (LEV * LAT_DEV)
    level = obs_row // LAT_DEV % LEV
    owner = jnp.arange(TILES, dtype=jnp.int32)[None, None, :, None]
    latitude = owner * LAT_DEV + obs_row % LAT_DEV
    window_of = jnp.broadcast_to(jnp.arange(SUBS, dtype=jnp.int32)[:, None, None, None], shaped)
    slots = jnp.arange(CAP, dtype=jnp.int32)[None, None, None, :]
    masked_weight = weights * (slots < obs_count[:, :, :, None]).astype(jnp.float32)

    def apply_forward(forcing):
        return forward_map(forcing, advect_east, advect_north, diffusion)
    shape_state = (SUBS, VARS, LEV, NLAT, LON)
    increment = jnp.zeros(shape_state, jnp.float32)
    for iteration in range(ITERS):
        states, pullback = jax.vjp(apply_forward, increment)
        picked = states[window_of, variable, level, latitude, obs_lon]
        innov = masked_weight * (picked - values)
        grad_obs = jnp.zeros(shape_state, jnp.float32).at[window_of, variable, level, latitude, obs_lon].add(innov)
        adjoint = pullback(grad_obs)[0]
        increment = increment - 0.5 * (increment + background_var * adjoint)
    return increment
```

```python
import functools

import jax
import jax.numpy as jnp
from jax import lax
from jax.experimental import pallas as pl
from jax.experimental.pallas import tpu as pltpu
from jax.sharding import PartitionSpec as P

MESH = pl.DeviceIdType.MESH
F32 = jnp.float32
BF16 = jnp.bfloat16
LON = 1440
LAT = 12
CAP = 32
FIELDS = 8
LANES = 256
GROUP = 2
HALO = 2 * GROUP
ROWS = LAT + 2 * HALO


def split3(value):
    high = value.astype(BF16).astype(F32)
    rest = value - high
    middle = rest.astype(BF16).astype(F32)
    return high, middle, rest - middle


def kernel(
    windows,
    tiles,
    coef_in,
    bv_in,
    obs_in,
    out_ref,
    obs1,
    obsall,
    craw,
    crawn,
    craws,
    der,
    bvr,
    hot,
    src,
    srcn,
    srcs,
    inc,
    incn,
    incs,
    states,
    final,
    carry,
    carryn,
    carrys,
    work,
    innov,
    innovl,
    innovr,
    obs_s,
    obs_r,
    ob2_s,
    ob2_r,
    c_s,
    c_r,
    ch_s,
    ch_r,
    bv_s,
    bv_r,
    src_s,
    src_r,
    inc_s,
    inc_r,
    car_s,
    car_r,
    inn_s,
    inn_r,
    out_s,
    out_r,
):
    m = lax.axis_index("tm")
    t = lax.axis_index("tile")
    chunk = LON // windows
    margin = (LANES - chunk) // 2
    groups = windows // GROUP
    slots = obsall.shape[-1]
    cells = LAT * FIELDS
    up = lax.rem(t + 1, tiles)
    down = lax.rem(t + tiles - 1, tiles)
    left = lax.rem(m + windows - 1, windows)
    right = lax.rem(m + 1, windows)
    edge_low = jnp.where(t == 0, 0.0, 1.0).astype(F32)
    edge_high = jnp.where(t == tiles - 1, 0.0, 1.0).astype(F32)

    barrier = pltpu.get_barrier_semaphore()

    def greet_tile(d, token):
        pl.semaphore_signal(
            barrier, inc=1, device_id=(m, lax.rem(t + d, tiles)), device_id_type=MESH
        )
        return token

    def greet_tm(d, token):
        pl.semaphore_signal(
            barrier, inc=1, device_id=(lax.rem(m + d, windows), t), device_id_type=MESH
        )
        return token

    lax.fori_loop(1, tiles, greet_tile, 0)
    lax.fori_loop(1, windows, greet_tm, 0)
    pl.semaphore_wait(barrier, tiles - 1 + windows - 1)

    def remote(source, target, send, recv, where):
        return pltpu.make_async_remote_copy(
            src_ref=source,
            dst_ref=target,
            send_sem=send,
            recv_sem=recv,
            device_id=where,
            device_id_type=MESH,
        )

    def obs_copy(d):
        peer = lax.rem(t + d, tiles)
        return remote(obs_in.at[peer], obs1.at[t], obs_s.at[d], obs_r.at[d], (m, peer))

    def obs_start(d, token):
        obs_copy(d).start()
        return token

    lax.fori_loop(1, tiles, obs_start, 0)

    coef_own = pltpu.make_async_copy(coef_in.at[m], craw.at[m], c_s.at[0])
    coef_own.start()
    bv_own = pltpu.make_async_copy(bv_in.at[m], bvr.at[m], bv_s.at[0])

    def coef_copy(d):
        peer = lax.rem(m + d, windows)
        return remote(coef_in.at[peer], craw.at[m], c_s.at[d], c_r.at[m], (peer, t))

    def bv_copy(d):
        peer = lax.rem(m + d, windows)
        return remote(bv_in.at[peer], bvr.at[m], bv_s.at[d], bv_r.at[m], (peer, t))

    def coef_start(d, token):
        coef_copy(d).start()
        return token

    lax.fori_loop(1, windows, coef_start, 0)

    for ref in (carry, carryn, carrys):
        for sweep in range(3):
            ref[sweep * groups] = jnp.zeros(ref.shape[1:], F32)

    obs1[t] = obs_in[t]

    def obs_wait(d, token):
        obs_copy(d).wait_recv()
        return token

    lax.fori_loop(1, tiles, obs_wait, 0)
    for j in range(tiles // 4):
        obsall[m, :, j * 128 : (j + 1) * 128] = (
            obs1[4 * j] + obs1[4 * j + 1] + obs1[4 * j + 2] + obs1[4 * j + 3]
        )

    def ob2_copy(d):
        peer = lax.rem(m + d, windows)
        return remote(obsall.at[m], obsall.at[m], ob2_s.at[d], ob2_r.at[m], (peer, t))

    def ob2_start(d, token):
        ob2_copy(d).start()
        return token

    lax.fori_loop(1, windows, ob2_start, 0)
    bv_own.start()

    def bv_start(d, token):
        bv_copy(d).start()
        return token

    lax.fori_loop(1, windows, bv_start, 0)

    def from_peer(ref, sem, k, own):
        @pl.when(k != m)
        def _():
            remote(ref.at[k], ref.at[k], sem.at[k], sem.at[k], (k, t)).wait_recv()

        if own is not None:

            @pl.when(k == m)
            def _():
                own.wait()

    edge_tiles = HALO * 6 // 8

    def coef_low(k):
        return remote(
            craw.at[k, 0:edge_tiles], craws.at[k], ch_s.at[0, k], ch_r.at[0, k], (m, down)
        )

    def coef_high(k):
        return remote(
            craw.at[k, 9 - edge_tiles : 9], crawn.at[k], ch_s.at[1, k], ch_r.at[1, k], (m, up)
        )

    def coef_forward(i, token):
        k = windows - 1 - i
        from_peer(craw, c_r, k, coef_own)
        coef_low(k).start()
        coef_high(k).start()
        return token

    lower = lax.broadcasted_iota(jnp.int32, (FIELDS, LANES), 0) < FIELDS // 2

    def expand(k):
        coef_low(k).wait_recv()
        coef_high(k).wait_recv()
        for r in range(ROWS):
            if r < HALO:
                ref, row, edge = crawn, r, edge_low
            elif r < HALO + LAT:
                ref, row, edge = craw, r - HALO, None
            else:
                ref, row, edge = craws, r - HALO - LAT, edge_high
            picked = []
            for c in range(3):
                q = (row * 3 + c) * 2
                one = ref[k, q // 8, q % 8 : q % 8 + 1, :]
                two = ref[k, q // 8, q % 8 + 1 : q % 8 + 2, :]
                picked.append(
                    jnp.where(
                        lower,
                        jnp.broadcast_to(one, (FIELDS, LANES)),
                        jnp.broadcast_to(two, (FIELDS, LANES)),
                    )
                )
            half_east, half_north, kap = 0.5 * picked[0], 0.5 * picked[1], picked[2]
            made = (
                1.0 - 4.0 * kap,
                kap - half_east,
                kap + half_east,
                kap - half_north,
                kap + half_north,
            )
            for c in range(5):
                der[k, c, r] = made[c] if edge is None else made[c] * edge

    base = m * chunk - margin

    def lane_of(k):
        rel = obsall[k, 1:2, :].astype(jnp.int32) - base
        rel = jnp.where(rel >= LON, rel - LON, rel)
        return jnp.where(rel < 0, rel + LON, rel)

    def make_hot(k):
        rel = lane_of(k)
        lanes = lax.broadcasted_iota(jnp.int32, (LANES, slots), 0)
        hot[k] = jnp.where(lanes == rel, 1.0, 0.0).astype(BF16)

    def row_mask(k):
        rows = lax.broadcasted_iota(jnp.int32, (cells, slots), 0)
        return rows == obsall[k, 0:1, :].astype(jnp.int32)

    def scatter(it, k, value):
        mask = row_mask(k)
        parts = [jnp.where(mask, part, 0.0).astype(BF16) for part in split3(value)]
        sums = lax.dot_general(
            jnp.concatenate(parts, axis=0),
            hot[k],
            (((1,), (1,)), ((), ())),
            preferred_element_type=F32,
        )
        total = sums[2 * cells :] + sums[cells : 2 * cells] + sums[:cells]
        src[it, k] = total.reshape(LAT, FIELDS, LANES)

    def src_low(it, k):
        return remote(
            src.at[it, pl.ds(k, GROUP), 0:HALO],
            srcs.at[it, pl.ds(k, GROUP)],
            src_s.at[it, 0, k // GROUP],
            src_r.at[it, 0, k // GROUP],
            (m, down),
        )

    def src_high(it, k):
        return remote(
            src.at[it, pl.ds(k, GROUP), LAT - HALO : LAT],
            srcn.at[it, pl.ds(k, GROUP)],
            src_s.at[it, 1, k // GROUP],
            src_r.at[it, 1, k // GROUP],
            (m, up),
        )

    def inc_low(k):
        return remote(
            inc.at[pl.ds(k, GROUP), 0:HALO],
            incs.at[pl.ds(k, GROUP)],
            inc_s.at[0, k // GROUP],
            inc_r.at[0, k // GROUP],
            (m, down),
        )

    def inc_high(k):
        return remote(
            inc.at[pl.ds(k, GROUP), LAT - HALO : LAT],
            incn.at[pl.ds(k, GROUP)],
            inc_s.at[1, k // GROUP],
            inc_r.at[1, k // GROUP],
            (m, up),
        )

    def carry_low(e):
        return remote(
            carry.at[e, 0:HALO], carrys.at[e], car_s.at[0, e], car_r.at[0, e], (m, down)
        )

    def carry_high(e):
        return remote(
            carry.at[e, LAT - HALO : LAT], carryn.at[e], car_s.at[1, e], car_r.at[1, e], (m, up)
        )

    def innov_left(k):
        return remote(
            innov.at[pl.ds(k, GROUP)],
            innovr.at[pl.ds(k, GROUP)],
            inn_s.at[0, k // GROUP],
            inn_r.at[0, k // GROUP],
            (left, t),
        )

    def innov_right(k):
        return remote(
            innov.at[pl.ds(k, GROUP)],
            innovl.at[pl.ds(k, GROUP)],
            inn_s.at[1, k // GROUP],
            inn_r.at[1, k // GROUP],
            (right, t),
        )

    def three(north, own, south, index, r):
        if r < HALO:
            return north[index + (r,)]
        if r < HALO + LAT:
            return own[index + (r - HALO,)]
        return south[index + (r - HALO - LAT,)]

    def adjoint_step(load, store, k, low, high):
        to_next = None
        held = None
        for r in range(low, high):
            x = load(r)
            south = der[k, 4, r] * x
            if held is not None and r - 1 >= low + 1:
                store(r - 1, held + south)
            if r < high - 1 and r > low:
                held = (
                    der[k, 0, r] * x
                    + pltpu.roll(der[k, 1, r] * x, 1, 1)
                    + pltpu.roll(der[k, 2, r] * x, LANES - 1, 1)
                    + to_next
                )
            to_next = der[k, 3, r] * x

    def forward_step(load, store, k, low, high):
        before, here = load(low), load(low + 1)
        for r in range(low + 1, high - 1):
            after = load(r + 1)
            store(
                r,
                der[k, 0, r] * here
                + der[k, 1, r] * pltpu.roll(here, LANES - 1, 1)
                + der[k, 2, r] * pltpu.roll(here, 1, 1)
                + der[k, 3, r] * after
                + der[k, 4, r] * before,
            )
            before, here = here, after

    def keep(slot):
        def store(r, value):
            work[slot, r] = value

        return store

    def wait_carry(i, e):
        @pl.when(i > 0)
        def _():
            carry_low(e).wait_recv()
            carry_high(e).wait_recv()

    def send_carry(i, e):
        @pl.when(i < groups - 1)
        def _():
            carry_low(e).start()
            carry_high(e).start()

    def adjoint_group(it, i, done):
        e = 2 * it * groups + i
        top = windows - 1 - GROUP * i
        src_low(it, top - GROUP + 1).wait_recv()
        src_high(it, top - GROUP + 1).wait_recv()
        wait_carry(i, e)
        for j in range(GROUP):
            k = top - j

            def load(r, j=j, k=k):
                if j == 0:
                    old = three(carryn, carry, carrys, (e,), r)
                else:
                    old = work[0, r]
                return old + three(srcn, src, srcs, (it, k), r)

            low, high = 2 * j, ROWS - 2 * j
            adjoint_step(load, keep(1), k, low, high)
            adjoint_step(lambda r: work[1, r], keep(0), k, low + 1, high - 1)
            if j == GROUP - 1:

                @pl.when(i < groups - 1)
                def _():
                    carry[e + 1] = work[0, HALO : HALO + LAT]

                send_carry(i, e + 1)
            done(k)

    lax.fori_loop(0, windows, coef_forward, 0)

    def prepare(i):
        for j in range(GROUP):
            k = windows - 1 - GROUP * i - j
            from_peer(obsall, ob2_r, k, None)
            make_hot(k)
            scatter(0, k, obsall[k, 3:4, :] * (0.0 - obsall[k, 2:3, :]))
        src_low(0, k).start()
        src_high(0, k).start()
        for j in range(GROUP):
            expand(windows - 1 - GROUP * i - j)

    prepare(0)

    def first(i, token):
        @pl.when(i < groups - 1)
        def _():
            prepare(i + 1)

        def done(k):
            from_peer(bvr, bv_r, k, bv_own)
            inc[k] = -0.5 * (bvr[k] * work[0, HALO : HALO + LAT])

        adjoint_group(0, i, done)
        k = windows - GROUP - GROUP * i
        inc_low(k).start()
        inc_high(k).start()
        return token

    lax.fori_loop(0, groups, first, 0)

    def observe(i):
        for j in range(GROUP):
            k = GROUP * i + j
            parts = split3(states[k].reshape(cells, LANES))
            picked = jnp.dot(
                jnp.concatenate([part.astype(BF16) for part in parts], axis=0),
                hot[k],
                preferred_element_type=F32,
            )
            total = picked[2 * cells :] + picked[cells : 2 * cells] + picked[:cells]
            seen = jnp.sum(jnp.where(row_mask(k), total, 0.0), axis=0, keepdims=True)
            rel = lane_of(k)
            own = (rel >= margin) & (rel < margin + chunk)
            innov[k] = jnp.where(own, obsall[k, 3:4, :] * (seen - obsall[k, 2:3, :]), 0.0)
        innov_left(GROUP * i).start()
        innov_right(GROUP * i).start()

    def second(i, token):
        @pl.when(i > 0)
        def _():
            observe(i - 1)

        e = groups + i
        inc_low(GROUP * i).wait_recv()
        inc_high(GROUP * i).wait_recv()
        wait_carry(i, e)
        for j in range(GROUP):
            k = GROUP * i + j

            def load(r, j=j, k=k):
                if j == 0:
                    old = three(carryn, carry, carrys, (e,), r)
                else:
                    old = work[0, r]
                total = old + three(incn, inc, incs, (k,), r)
                if r < HALO:
                    return total * edge_low
                if r >= HALO + LAT:
                    return total * edge_high
                return total

            low, high = 2 * j, ROWS - 2 * j
            forward_step(load, keep(1), k, low, high)
            forward_step(lambda r: work[1, r], keep(0), k, low + 1, high - 1)
            if j == GROUP - 1:

                @pl.when(i < groups - 1)
                def _():
                    carry[e + 1] = work[0, HALO : HALO + LAT]

                send_carry(i, e + 1)
            states[k] = work[0, HALO : HALO + LAT]
        return token

    lax.fori_loop(0, groups, second, 0)
    observe(groups - 1)

    def regrid(i):
        k = windows - GROUP - GROUP * i
        innov_left(k).wait_recv()
        innov_right(k).wait_recv()
        for j in range(GROUP):
            scatter(1, k + j, innov[k + j] + innovl[k + j] + innovr[k + j])
        src_low(1, k).start()
        src_high(1, k).start()

    regrid(0)

    def out_copy(k):
        return remote(final.at[k], out_ref.at[m], out_s.at[k], out_r.at[m], (k, t))

    out_own = pltpu.make_async_copy(final.at[m], out_ref.at[m], out_s.at[m])

    def third(i, token):
        @pl.when(i < groups - 1)
        def _():
            regrid(i + 1)

        def done(k):
            old = inc[k]
            final[k] = old - 0.5 * (old + bvr[k] * work[0, HALO : HALO + LAT])

            @pl.when(k != m)
            def _():
                out_copy(k).start()

            @pl.when(k == m)
            def _():
                out_own.start()

        adjoint_group(1, i, done)
        return token

    lax.fori_loop(0, groups, third, 0)

    def finish_obs(d, token):
        obs_copy(d).wait_send()
        return token

    lax.fori_loop(1, tiles, finish_obs, 0)

    def finish_tm(d, token):
        coef_copy(d).wait_send()
        bv_copy(d).wait_send()
        ob2_copy(d).wait_send()
        return token

    lax.fori_loop(1, windows, finish_tm, 0)

    def finish_windows(k, token):
        coef_low(k).wait_send()
        coef_high(k).wait_send()

        @pl.when(k != m)
        def _():
            out_copy(k).wait_send()
            remote(final.at[k], out_ref.at[k], out_s.at[k], out_r.at[k], (k, t)).wait_recv()

        @pl.when(k == m)
        def _():
            out_own.wait()

        return token

    lax.fori_loop(0, windows, finish_windows, 0)

    def finish_groups(i, token):
        k = GROUP * i
        for it in range(2):
            src_low(it, k).wait_send()
            src_high(it, k).wait_send()
        inc_low(k).wait_send()
        inc_high(k).wait_send()
        innov_left(k).wait_send()
        innov_right(k).wait_send()

        @pl.when(i > 0)
        def _():
            for sweep in range(3):
                carry_low(sweep * groups + i).wait_send()
                carry_high(sweep * groups + i).wait_send()

        return token

    lax.fori_loop(0, groups, finish_groups, 0)


def per_device(
    advect_east, advect_north, diffusion, background_var, obs_cell, obs_value, obs_weight, obs_count
):
    windows = lax.axis_size("tm")
    tiles = lax.axis_size("tile")
    groups = windows // GROUP
    chunk = LON // windows
    margin = (LANES - chunk) // 2
    slots = tiles * CAP
    tile = lax.axis_index("tile")

    def chunks(array):
        wide = jnp.concatenate([array[..., -margin:], array, array[..., :margin]], axis=-1)
        return jnp.stack([wide[..., c * chunk : c * chunk + LANES] for c in range(windows)])

    coefs = jnp.stack([advect_east[0], advect_north[0], diffusion[0]])
    coefs = chunks(coefs.transpose(2, 0, 1, 3).reshape(LAT * 6, LON))
    coefs = coefs.reshape(windows, LAT * 6 // 8, 8, LANES)
    variances = chunks(background_var[0].transpose(2, 1, 0, 3).reshape(LAT, FIELDS, LON))

    cell = obs_cell.reshape(tiles, CAP)
    live = jnp.arange(CAP, dtype=jnp.int32)[None, :] < obs_count.reshape(tiles)[:, None]
    masked = obs_weight.reshape(tiles, CAP) * live.astype(F32)
    row, lon = cell // LON, cell % LON
    variable, level, latitude = row // (2 * LAT), row // LAT % 2, row % LAT
    place = latitude * FIELDS + level * (FIELDS // 2) + variable
    packed = jnp.stack(
        [place.astype(F32), lon.astype(F32), obs_value.reshape(tiles, CAP), masked], axis=1
    )
    quarter = jnp.arange(128, dtype=jnp.int32) // CAP == lax.rem(tile, 4)
    packed = jnp.where(quarter, jnp.tile(packed, (1, 1, 128 // CAP)), 0.0)

    field = (FIELDS, LANES)
    dma = pltpu.SemaphoreType.DMA
    out = pl.pallas_call(
        functools.partial(kernel, windows, tiles),
        out_shape=jax.ShapeDtypeStruct((windows, LAT) + field, F32),
        in_specs=[
            pl.BlockSpec(memory_space=pl.ANY),
            pl.BlockSpec(memory_space=pl.ANY),
            pl.BlockSpec(memory_space=pltpu.VMEM),
        ],
        out_specs=pl.BlockSpec(memory_space=pl.ANY),
        scratch_shapes=[
            pltpu.VMEM((tiles, 4, 128), F32),
            pltpu.VMEM((windows, 4, slots), F32),
            pltpu.VMEM((windows, LAT * 6 // 8, 8, LANES), F32),
            pltpu.VMEM((windows, HALO * 6 // 8, 8, LANES), F32),
            pltpu.VMEM((windows, HALO * 6 // 8, 8, LANES), F32),
            pltpu.VMEM((windows, 5, ROWS) + field, F32),
            pltpu.VMEM((windows, LAT) + field, F32),
            pltpu.VMEM((windows, LANES, slots), BF16),
            pltpu.VMEM((2, windows, LAT) + field, F32),
            pltpu.VMEM((2, windows, HALO) + field, F32),
            pltpu.VMEM((2, windows, HALO) + field, F32),
            pltpu.VMEM((windows, LAT) + field, F32),
            pltpu.VMEM((windows, HALO) + field, F32),
            pltpu.VMEM((windows, HALO) + field, F32),
            pltpu.VMEM((windows, LAT) + field, F32),
            pltpu.VMEM((windows, LAT) + field, F32),
            pltpu.VMEM((3 * groups, LAT) + field, F32),
            pltpu.VMEM((3 * groups, HALO) + field, F32),
            pltpu.VMEM((3 * groups, HALO) + field, F32),
            pltpu.VMEM((2, ROWS) + field, F32),
            pltpu.VMEM((windows, 1, slots), F32),
            pltpu.VMEM((windows, 1, slots), F32),
            pltpu.VMEM((windows, 1, slots), F32),
            dma((tiles,)),
            dma((tiles,)),
            dma((windows,)),
            dma((windows,)),
            dma((windows,)),
            dma((windows,)),
            dma((2, windows)),
            dma((2, windows)),
            dma((windows,)),
            dma((windows,)),
            dma((2, 2, groups)),
            dma((2, 2, groups)),
            dma((2, groups)),
            dma((2, groups)),
            dma((2, 3 * groups)),
            dma((2, 3 * groups)),
            dma((2, groups)),
            dma((2, groups)),
            dma((windows,)),
            dma((windows,)),
        ],
        compiler_params=pltpu.CompilerParams(
            collective_id=0, has_side_effects=True, vmem_limit_bytes=48 * 1024 * 1024
        ),
    )(coefs, variances, packed)
    own = out[..., margin : margin + chunk].reshape(windows, LAT, 2, 4, chunk)
    return own.transpose(3, 2, 1, 0, 4).reshape(1, 4, 2, LAT, LON)


def solution(mesh):
    return jax.shard_map(
        per_device,
        mesh=mesh,
        in_specs=(
            P("tm", None, "tile", None),
            P("tm", None, "tile", None),
            P("tm", None, "tile", None),
            P("tm", None, None, "tile", None),
            P("tm", "tile", None),
            P("tm", "tile", None),
            P("tm", "tile", None),
            P("tm", "tile", None),
        ),
        out_specs=P("tm", None, None, "tile", None),
        check_vma=False,
    )
```

```python
import functools

import jax
import jax.numpy as jnp
from jax import lax
from jax.experimental import pallas as pl
from jax.experimental.pallas import tpu as pltpu
from jax.sharding import PartitionSpec as P

MESH = pl.DeviceIdType.MESH
F32 = jnp.float32
BF16 = jnp.bfloat16
LON = 1440
LAT = 12
CAP = 32
FIELDS = 8
LANES = 256
GROUP = 4
HALO = 2 * GROUP
ROWS = LAT + 2 * HALO
REACH = [max(2 * (GROUP - j) - 1, 2 * (j + 1)) for j in range(GROUP)]


def split3(value):
    high = value.astype(BF16).astype(F32)
    rest = value - high
    middle = rest.astype(BF16).astype(F32)
    return high, middle, rest - middle


def kernel(
    windows,
    tiles,
    coef_in,
    bv_in,
    cell_in,
    value_in,
    weight_in,
    count_in,
    out_ref,
    obs0,
    obs1,
    obsall,
    craw,
    crawn,
    craws,
    der,
    bvraw,
    bvpack,
    bvr,
    hot,
    src,
    inc,
    incn,
    incs,
    states,
    final,
    carry,
    carryn,
    carrys,
    result,
    work,
    innov,
    arrived,
    obs_s,
    obs_r,
    ob2_s,
    ob2_r,
    c_s,
    c_r,
    ch_s,
    ch_r,
    raw_s,
    bv_s,
    bv_r,
    inc_s,
    inc_r,
    car_s,
    car_r,
    inn_s,
    inn_r,
    out_s,
    out_r,
):
    m = lax.axis_index("tm")
    t = lax.axis_index("tile")
    chunk = LON // windows
    margin = (LANES - chunk) // 2
    groups = windows // GROUP
    slots = obsall.shape[-1]
    cells = LAT * FIELDS
    up = lax.rem(t + 1, tiles)
    down = lax.rem(t + tiles - 1, tiles)
    left = lax.rem(m + windows - 1, windows)
    right = lax.rem(m + 1, windows)
    edge_low = jnp.where(t == 0, 0.0, 1.0).astype(F32)
    edge_high = jnp.where(t == tiles - 1, 0.0, 1.0).astype(F32)

    barrier = pltpu.get_barrier_semaphore()

    def greet_tile(d, token):
        pl.semaphore_signal(
            barrier, inc=1, device_id=(m, lax.rem(t + d, tiles)), device_id_type=MESH
        )
        return token

    def greet_tm(d, token):
        for where in (t, down, up):
            pl.semaphore_signal(
                barrier, inc=1, device_id=(lax.rem(m + d, windows), where), device_id_type=MESH
            )
        return token

    lax.fori_loop(1, tiles, greet_tile, 0)
    lax.fori_loop(1, windows, greet_tm, 0)

    raw_copy = pltpu.make_async_copy(bv_in, bvraw, raw_s)
    raw_copy.start()
    lane = lax.broadcasted_iota(jnp.int32, (1, 128), 1)
    quarter = lane // CAP
    slot = lane - CAP * quarter
    mine = lax.rem(t, 4)

    def floor_div(value, by):
        return jnp.floor((value + 0.5) * (1.0 / by))

    for a in range(tiles // 4):
        part = slice(a * 128, (a + 1) * 128)
        cell = cell_in[0:1, part].astype(F32)
        row = floor_div(cell, LON)
        lon = cell - LON * row
        variable = floor_div(row, 2 * LAT)
        rest = row - 2 * LAT * variable
        level = floor_div(rest, LAT)
        place = FIELDS * (rest - LAT * level) + 2 * variable + level
        filled = jnp.where(
            quarter < 2,
            jnp.where(quarter == 0, count_in[0, 4 * a], count_in[0, 4 * a + 1]),
            jnp.where(quarter == 2, count_in[0, 4 * a + 2], count_in[0, 4 * a + 3]),
        )
        weight = jnp.where(slot < filled, weight_in[0:1, part], 0.0)
        block = jnp.concatenate(
            [place * LON + lon, value_in[0:1, part], weight, jnp.zeros((1, 128), F32)], axis=0
        )
        for b in range(4):
            turned = pltpu.roll(block, CAP * lax.rem(mine + 4 - b, 4), 1)
            obs0[4 * a + b] = jnp.where(quarter == mine, turned, 0.0)

    for ref in (carry, carryn, carrys):
        for sweep in range(3):
            ref[sweep * groups] = jnp.zeros(ref.shape[1:], F32)

    pl.semaphore_wait(barrier, tiles - 1 + 3 * (windows - 1))

    def remote(source, target, send, recv, where):
        return pltpu.make_async_remote_copy(
            src_ref=source,
            dst_ref=target,
            send_sem=send,
            recv_sem=recv,
            device_id=where,
            device_id_type=MESH,
        )

    def obs_copy(d):
        peer = lax.rem(t + d, tiles)
        return remote(obs0.at[peer], obs1.at[t], obs_s.at[d], obs_r.at[d], (m, peer))

    def obs_start(d, token):
        obs_copy(d).start()
        return token

    lax.fori_loop(1, tiles, obs_start, 0)

    coef_own = pltpu.make_async_copy(coef_in.at[m], craw.at[m], c_s.at[0])
    coef_own.start()

    def coef_copy(d):
        peer = lax.rem(m + d, windows)
        return remote(coef_in.at[peer], craw.at[m], c_s.at[d], c_r.at[m], (peer, t))

    def bv_copy(d):
        peer = lax.rem(m + d, windows)
        return remote(bvpack.at[peer], bvr.at[m], bv_s.at[d], bv_r.at[m], (peer, t))

    def coef_start(d, token):
        coef_copy(d).start()
        return token

    lax.fori_loop(1, windows, coef_start, 0)

    raw_copy.wait()
    for c in range(windows):
        start = c * chunk - margin
        for r in range(LAT):
            if start < 0:
                piece = jnp.concatenate(
                    [bvraw[:, r, LON + start : LON], bvraw[:, r, 0 : LANES + start]], axis=1
                )
            elif start + LANES > LON:
                piece = jnp.concatenate(
                    [bvraw[:, r, start:LON], bvraw[:, r, 0 : start + LANES - LON]], axis=1
                )
            else:
                piece = bvraw[:, r, start : start + LANES]
            bvpack[c, r] = piece
    bvr[m] = bvpack[m]

    obs1[t] = obs0[t]

    def obs_wait(d, token):
        obs_copy(d).wait_recv()
        return token

    lax.fori_loop(1, tiles, obs_wait, 0)
    for j in range(tiles // 4):
        merged = obs1[4 * j] + obs1[4 * j + 1] + obs1[4 * j + 2] + obs1[4 * j + 3]
        for c in range(3):
            obsall[m, 0, c, :, j * 128 : (j + 1) * 128] = merged[c : c + 1]

    def ob2_copy(d, n):
        peer = lax.rem(m + d, windows)
        where = (t, up, down)[n]
        return remote(
            obsall.at[m, 0], obsall.at[m, n], ob2_s.at[n, d], ob2_r.at[n, m], (peer, where)
        )

    def ob2_start(d, token):
        for n in range(3):
            ob2_copy(d, n).start()
        return token

    for n in (1, 2):
        ob2_copy(0, n).start()
    lax.fori_loop(1, windows, ob2_start, 0)

    def bv_start(d, token):
        bv_copy(d).start()
        return token

    lax.fori_loop(1, windows, bv_start, 0)

    def from_peer(ref, sem, k, own):
        @pl.when(k != m)
        def _():
            remote(ref.at[k], ref.at[k], sem.at[k], sem.at[k], (k, t)).wait_recv()

        if own is not None:

            @pl.when(k == m)
            def _():
                own.wait()

    whole = LAT * 6 // 8
    edge_tiles = HALO * 6 // 8

    def coef_low(k, j):
        size = -(-REACH[j] * 6 // 8)
        return remote(
            craw.at[k, 0:size], craws.at[k, 0:size], ch_s.at[0, k], ch_r.at[0, k], (m, down)
        )

    def coef_high(k, j):
        size = -(-REACH[j] * 6 // 8)
        return remote(
            craw.at[k, whole - size : whole],
            crawn.at[k, edge_tiles - size : edge_tiles],
            ch_s.at[1, k],
            ch_r.at[1, k],
            (m, up),
        )

    def coef_forward(i, token):
        for j in range(GROUP - 1, -1, -1):
            k = windows - GROUP - GROUP * i + j
            from_peer(craw, c_r, k, coef_own)
            coef_low(k, j).start()
            coef_high(k, j).start()
        return token

    even = lax.rem(lax.broadcasted_iota(jnp.int32, (FIELDS, LANES), 0), 2) == 0

    def expand(k, j):
        coef_low(k, j).wait_recv()
        coef_high(k, j).wait_recv()
        for r in range(HALO - REACH[j], HALO + LAT + REACH[j]):
            if r < HALO:
                ref, row, edge = crawn, r, edge_low
            elif r < HALO + LAT:
                ref, row, edge = craw, r - HALO, None
            else:
                ref, row, edge = craws, r - HALO - LAT, edge_high
            picked = []
            for c in range(3):
                q = (row * 3 + c) * 2
                one = ref[k, q // 8, q % 8 : q % 8 + 1, :]
                two = ref[k, q // 8, q % 8 + 1 : q % 8 + 2, :]
                picked.append(
                    jnp.where(
                        even,
                        jnp.broadcast_to(one, (FIELDS, LANES)),
                        jnp.broadcast_to(two, (FIELDS, LANES)),
                    )
                )
            half_east, half_north, kap = 0.5 * picked[0], 0.5 * picked[1], picked[2]
            made = (
                1.0 - 4.0 * kap,
                kap - half_east,
                kap + half_east,
                kap - half_north,
                kap + half_north,
            )
            for c in range(5):
                der[k, c, r] = made[c] if edge is None else made[c] * edge

    base = m * chunk - margin

    def place_and_lane(k, n):
        code = obsall[k, n, 0]
        place = floor_div(code, LON)
        rel = (code - LON * place).astype(jnp.int32) - base
        rel = jnp.where(rel >= LON, rel - LON, rel)
        return place.astype(jnp.int32), jnp.where(rel < 0, rel + LON, rel)

    def make_hot(k, n):
        place, rel = place_and_lane(k, n)
        lanes = lax.broadcasted_iota(jnp.int32, (LANES, slots), 0)
        hot[k, n] = jnp.where(lanes == rel, 1.0, 0.0).astype(BF16)

    def row_mask(k, n, first, count):
        place, rel = place_and_lane(k, n)
        rows = lax.broadcasted_iota(jnp.int32, (count * FIELDS, slots), 0) + first * FIELDS
        return rows == place

    def scatter(it, k, j, value_of):
        reach = 2 * (j + 1)
        for n, first, count, to in (
            (0, 0, LAT, HALO),
            (1, LAT - reach, reach, HALO - reach),
            (2, 0, reach, HALO + LAT),
        ):
            mask = row_mask(k, n, first, count)
            parts = [jnp.where(mask, part, 0.0).astype(BF16) for part in split3(value_of(n))]
            sums = lax.dot_general(
                jnp.concatenate(parts, axis=0),
                hot[k, n],
                (((1,), (1,)), ((), ())),
                preferred_element_type=F32,
            )
            size = count * FIELDS
            total = sums[2 * size :] + sums[size : 2 * size] + sums[:size]
            src[it, k, to : to + count] = total.reshape(count, FIELDS, LANES)

    def inc_low(k, j):
        size = HALO - 2 * j
        return remote(
            inc.at[k, 0:size], incs.at[k, 0:size], inc_s.at[0, k], inc_r.at[0, k], (m, down)
        )

    def inc_high(k, j):
        size = HALO - 2 * j
        return remote(
            inc.at[k, LAT - size : LAT],
            incn.at[k, HALO - size : HALO],
            inc_s.at[1, k],
            inc_r.at[1, k],
            (m, up),
        )

    def carry_low(e):
        return remote(
            carry.at[e, 0:HALO], carrys.at[e], car_s.at[0, e], car_r.at[0, e], (m, down)
        )

    def carry_high(e):
        return remote(
            carry.at[e, LAT - HALO : LAT], carryn.at[e], car_s.at[1, e], car_r.at[1, e], (m, up)
        )

    steps = [(a, b) for a in (0, -1, 1) for b in (0, 1, -1)][1:]

    def innov_copy(k, n):
        a, b = steps[n]
        return remote(
            innov.at[pl.ds(k, GROUP)],
            arrived.at[n, pl.ds(k, GROUP)],
            inn_s.at[n, k // GROUP],
            inn_r.at[n, k // GROUP],
            ((left, m, right)[a + 1], (down, t, up)[b + 1]),
        )

    def three(north, own, south, index, r):
        if r < HALO:
            return north[index + (r,)]
        if r < HALO + LAT:
            return own[index + (r - HALO,)]
        return south[index + (r - HALO - LAT,)]

    def adjoint_step(load, store, k, low, high):
        to_next = None
        held = None
        for r in range(low, high):
            x = load(r)
            south = der[k, 4, r] * x
            if held is not None and r - 1 >= low + 1:
                store(r - 1, held + south)
            if r < high - 1 and r > low:
                held = (
                    der[k, 0, r] * x
                    + pltpu.roll(der[k, 1, r] * x, 1, 1)
                    + pltpu.roll(der[k, 2, r] * x, LANES - 1, 1)
                    + to_next
                )
            to_next = der[k, 3, r] * x

    def forward_step(load, store, k, low, high):
        before, here = load(low), load(low + 1)
        for r in range(low + 1, high - 1):
            after = load(r + 1)
            store(
                r,
                der[k, 0, r] * here
                + der[k, 1, r] * pltpu.roll(here, LANES - 1, 1)
                + der[k, 2, r] * pltpu.roll(here, 1, 1)
                + der[k, 3, r] * after
                + der[k, 4, r] * before,
            )
            before, here = here, after

    def keep(slot):
        def store(r, value):
            work[slot, r] = value

        return store

    def wait_carry(i, e):
        @pl.when(i > 0)
        def _():
            carry_low(e).wait_recv()
            carry_high(e).wait_recv()

    def send_carry(i, e):
        @pl.when(i < groups - 1)
        def _():
            carry_low(e).start()
            carry_high(e).start()

    def adjoint_group(it, i, done):
        e = 2 * it * groups + i
        top = windows - 1 - GROUP * i
        wait_carry(i, e)
        for j in range(GROUP):
            k = top - j

            def load(r, j=j, k=k):
                if j == 0:
                    old = three(carryn, carry, carrys, (e,), r)
                else:
                    old = work[0, r]
                return old + src[it, k, r]

            low, high = 2 * j, ROWS - 2 * j
            adjoint_step(load, keep(1), k, low, high)
            adjoint_step(lambda r: work[1, r], keep(0), k, low + 1, high - 1)
            if j == GROUP - 1:

                @pl.when(i < groups - 1)
                def _():
                    carry[e + 1] = work[0, HALO : HALO + LAT]

                send_carry(i, e + 1)
            done(k)

    lax.fori_loop(0, groups, coef_forward, 0)

    def prepare(i):
        for j in range(GROUP - 1, -1, -1):
            k = windows - GROUP - GROUP * i + j
            for n in range(3):
                sem = ob2_r.at[n, k]
                if n == 0:

                    @pl.when(k != m)
                    def _(k=k, sem=sem):
                        remote(
                            obsall.at[k, 0], obsall.at[k, 0], sem, sem, (k, t)
                        ).wait_recv()

                else:
                    remote(
                        obsall.at[k, n], obsall.at[k, n], sem, sem, (k, (down, up)[n - 1])
                    ).wait_recv()
                make_hot(k, n)
            scatter(0, k, j, lambda n, k=k: obsall[k, n, 2] * (0.0 - obsall[k, n, 1]))
        for j in range(GROUP - 1, -1, -1):
            expand(windows - GROUP - GROUP * i + j, j)

    prepare(0)

    def increments(i):
        for j in range(GROUP):
            k = windows - GROUP - GROUP * i + j
            from_peer(bvr, bv_r, k, None)
            inc[k] = -0.5 * (bvr[k] * inc[k])
            inc_low(k, j).start()
            inc_high(k, j).start()

    def first(i, token):
        @pl.when(i < groups - 1)
        def _():
            prepare(i + 1)

        @pl.when(i > 0)
        def _():
            increments(i - 1)

        def done(k):
            inc[k] = work[0, HALO : HALO + LAT]

        adjoint_group(0, i, done)
        return token

    lax.fori_loop(0, groups, first, 0)
    increments(groups - 1)

    def observe(i):
        for j in range(GROUP):
            k = GROUP * i + j
            parts = split3(states[k].reshape(cells, LANES))
            picked = jnp.dot(
                jnp.concatenate([part.astype(BF16) for part in parts], axis=0),
                hot[k, 0],
                preferred_element_type=F32,
            )
            total = picked[2 * cells :] + picked[cells : 2 * cells] + picked[:cells]
            seen = jnp.sum(jnp.where(row_mask(k, 0, 0, LAT), total, 0.0), axis=0, keepdims=True)
            place, rel = place_and_lane(k, 0)
            own = (rel >= margin) & (rel < margin + chunk)
            innov[k] = jnp.where(own, obsall[k, 0, 2] * (seen - obsall[k, 0, 1]), 0.0)
        for n in range(8):
            innov_copy(GROUP * i, n).start()

    def second(i, token):
        @pl.when(i > 0)
        def _():
            observe(i - 1)

        e = groups + i
        wait_carry(i, e)
        for j in range(GROUP):
            k = GROUP * i + j
            inc_low(k, j).wait_recv()
            inc_high(k, j).wait_recv()

            def load(r, j=j, k=k):
                if j == 0:
                    old = three(carryn, carry, carrys, (e,), r)
                else:
                    old = work[0, r]
                total = old + three(incn, inc, incs, (k,), r)
                if r < HALO:
                    return total * edge_low
                if r >= HALO + LAT:
                    return total * edge_high
                return total

            low, high = 2 * j, ROWS - 2 * j
            forward_step(load, keep(1), k, low, high)
            forward_step(lambda r: work[1, r], keep(0), k, low + 1, high - 1)
            if j == GROUP - 1:

                @pl.when(i < groups - 1)
                def _():
                    carry[e + 1] = work[0, HALO : HALO + LAT]

                send_carry(i, e + 1)
            states[k] = work[0, HALO : HALO + LAT]
        return token

    lax.fori_loop(0, groups, second, 0)
    observe(groups - 1)

    def regrid(i):
        k = windows - GROUP - GROUP * i
        for n in range(8):
            innov_copy(k, n).wait_recv()

        def total(n, k):
            b = (0, 1, -1)[n]
            found = [arrived[x, k] for x in range(8) if steps[x][1] == b]
            if n == 0:
                found.append(innov[k])
            return found[0] + found[1] + found[2]

        for j in range(GROUP - 1, -1, -1):
            scatter(1, k + j, j, lambda n, k=k + j: total(n, k))

    regrid(0)

    def out_copy(k):
        return remote(final.at[k], result.at[m], out_s.at[k], out_r.at[m], (k, t))


    def third(i, token):
        @pl.when(i < groups - 1)
        def _():
            regrid(i + 1)

        def done(k):
            old = inc[k]
            final[k] = old - 0.5 * (old + bvr[k] * work[0, HALO : HALO + LAT])

            @pl.when(k != m)
            def _():
                out_copy(k).start()

            @pl.when(k == m)
            def _():
                result[k] = final[k]

        adjoint_group(1, i, done)
        return token

    lax.fori_loop(0, groups, third, 0)

    def finish_obs(d, token):
        obs_copy(d).wait_send()
        return token

    lax.fori_loop(1, tiles, finish_obs, 0)

    def finish_tm(d, token):
        coef_copy(d).wait_send()
        bv_copy(d).wait_send()
        for n in range(3):
            ob2_copy(d, n).wait_send()
        return token

    for n in (1, 2):
        ob2_copy(0, n).wait_send()
    lax.fori_loop(1, windows, finish_tm, 0)

    def finish_groups(i, token):
        for j in range(GROUP):
            k = GROUP * i + j
            coef_low(k, j).wait_send()
            coef_high(k, j).wait_send()
            inc_low(k, j).wait_send()
            inc_high(k, j).wait_send()
        for n in range(8):
            innov_copy(GROUP * i, n).wait_send()

        @pl.when(i > 0)
        def _():
            for sweep in range(3):
                carry_low(sweep * groups + i).wait_send()
                carry_high(sweep * groups + i).wait_send()

        return token

    lax.fori_loop(0, groups, finish_groups, 0)

    def finish_windows(k, token):
        @pl.when(k != m)
        def _():
            remote(final.at[k], result.at[k], out_s.at[k], out_r.at[k], (k, t)).wait_recv()
            out_copy(k).wait_send()

        return token

    lax.fori_loop(0, windows, finish_windows, 0)
    for r in range(LAT):
        out_ref[:, r, :] = jnp.concatenate(
            [result[c, r, :, margin : margin + chunk] for c in range(windows)], axis=1
        )


def per_device(
    advect_east, advect_north, diffusion, background_var, obs_cell, obs_value, obs_weight, obs_count
):
    windows = lax.axis_size("tm")
    tiles = lax.axis_size("tile")
    groups = windows // GROUP
    chunk = LON // windows
    margin = (LANES - chunk) // 2
    slots = tiles * CAP

    def chunks(array):
        wide = jnp.concatenate([array[..., -margin:], array, array[..., :margin]], axis=-1)
        return jnp.stack([wide[..., c * chunk : c * chunk + LANES] for c in range(windows)])

    coefs = jnp.stack([advect_east[0], advect_north[0], diffusion[0]])
    coefs = chunks(coefs.transpose(2, 0, 1, 3).reshape(LAT * 6, LON))
    coefs = coefs.reshape(windows, LAT * 6 // 8, 8, LANES)
    field = (FIELDS, LANES)
    dma = pltpu.SemaphoreType.DMA
    out = pl.pallas_call(
        functools.partial(kernel, windows, tiles),
        out_shape=jax.ShapeDtypeStruct((FIELDS, LAT, LON), F32),
        in_specs=[
            pl.BlockSpec(memory_space=pl.ANY),
            pl.BlockSpec(memory_space=pl.ANY),
            pl.BlockSpec(memory_space=pltpu.VMEM),
            pl.BlockSpec(memory_space=pltpu.VMEM),
            pl.BlockSpec(memory_space=pltpu.VMEM),
            pl.BlockSpec(memory_space=pltpu.SMEM),
        ],
        out_specs=pl.BlockSpec(memory_space=pltpu.VMEM),
        scratch_shapes=[
            pltpu.VMEM((tiles, 4, 128), F32),
            pltpu.VMEM((tiles, 4, 128), F32),
            pltpu.VMEM((windows, 3, 3, 1, slots), F32),
            pltpu.VMEM((windows, LAT * 6 // 8, 8, LANES), F32),
            pltpu.VMEM((windows, HALO * 6 // 8, 8, LANES), F32),
            pltpu.VMEM((windows, HALO * 6 // 8, 8, LANES), F32),
            pltpu.VMEM((windows, 5, ROWS) + field, F32),
            pltpu.VMEM((FIELDS, LAT, LON), F32),
            pltpu.VMEM((windows, LAT) + field, F32),
            pltpu.VMEM((windows, LAT) + field, F32),
            pltpu.VMEM((windows, 3, LANES, slots), BF16),
            pltpu.VMEM((2, windows, ROWS) + field, F32),
            pltpu.VMEM((windows, LAT) + field, F32),
            pltpu.VMEM((windows, HALO) + field, F32),
            pltpu.VMEM((windows, HALO) + field, F32),
            pltpu.VMEM((windows, LAT) + field, F32),
            pltpu.VMEM((windows, LAT) + field, F32),
            pltpu.VMEM((3 * groups, LAT) + field, F32),
            pltpu.VMEM((3 * groups, HALO) + field, F32),
            pltpu.VMEM((3 * groups, HALO) + field, F32),
            pltpu.VMEM((windows, LAT) + field, F32),
            pltpu.VMEM((2, ROWS) + field, F32),
            pltpu.VMEM((windows, 1, slots), F32),
            pltpu.VMEM((8, windows, 1, slots), F32),
            dma((tiles,)),
            dma((tiles,)),
            dma((3, windows)),
            dma((3, windows)),
            dma((windows,)),
            dma((windows,)),
            dma((2, windows)),
            dma((2, windows)),
            dma,
            dma((windows,)),
            dma((windows,)),
            dma((2, windows)),
            dma((2, windows)),
            dma((2, 3 * groups)),
            dma((2, 3 * groups)),
            dma((8, groups)),
            dma((8, groups)),
            dma((windows,)),
            dma((windows,)),
        ],
        compiler_params=pltpu.CompilerParams(
            collective_id=0, has_side_effects=True, vmem_limit_bytes=48 * 1024 * 1024
        ),
    )(
        coefs,
        background_var.reshape(FIELDS, LAT, LON),
        obs_cell.reshape(1, slots),
        obs_value.reshape(1, slots),
        obs_weight.reshape(1, slots),
        obs_count.reshape(1, tiles),
    )
    return out.reshape(1, FIELDS // 2, 2, LAT, LON)


def solution(mesh):
    return jax.shard_map(
        per_device,
        mesh=mesh,
        in_specs=(
            P("tm", None, "tile", None),
            P("tm", None, "tile", None),
            P("tm", None, "tile", None),
            P("tm", None, None, "tile", None),
            P("tm", "tile", None),
            P("tm", "tile", None),
            P("tm", "tile", None),
            P("tm", "tile", None),
        ),
        out_specs=P("tm", None, None, "tile", None),
        check_vma=False,
    )
```

```python
import functools

import jax
import jax.numpy as jnp
from jax import lax
from jax.experimental import pallas as pl
from jax.experimental.pallas import tpu as pltpu
from jax.sharding import PartitionSpec as P

MESH = pl.DeviceIdType.MESH
F32 = jnp.float32
BF16 = jnp.bfloat16
LON = 1440
LAT = 12
CAP = 32
FIELDS = 8
LANES = 256
GROUP = 4
HALO = 2 * GROUP
ROWS = LAT + 2 * HALO
REACH = [max(2 * (GROUP - j) - 1, 2 * (j + 1)) for j in range(GROUP)]


def split3(value):
    high = value.astype(BF16).astype(F32)
    rest = value - high
    middle = rest.astype(BF16).astype(F32)
    return high, middle, rest - middle


def kernel(
    windows,
    tiles,
    east_hbm,
    north_hbm,
    diff_hbm,
    bv_hbm,
    cell_hbm,
    value_hbm,
    weight_hbm,
    count_hbm,
    out_ref,
    coef3,
    coef72,
    coef_in,
    cell_in,
    value_in,
    weight_in,
    count_in,
    obs0,
    obs1,
    obsall,
    craw,
    crawn,
    craws,
    der,
    bvraw,
    bvpack,
    bvr,
    hot,
    src,
    inc,
    incn,
    incs,
    states,
    final,
    carry,
    carryn,
    carrys,
    result,
    work,
    innov,
    arrived,
    obs_s,
    obs_r,
    ob2_s,
    ob2_r,
    c_s,
    c_r,
    ch_s,
    ch_r,
    raw_s,
    bv_s,
    bv_r,
    inc_s,
    inc_r,
    car_s,
    car_r,
    inn_s,
    inn_r,
    out_s,
    out_r,
):
    m = lax.axis_index("tm")
    t = lax.axis_index("tile")
    chunk = LON // windows
    margin = (LANES - chunk) // 2
    groups = windows // GROUP
    slots = obsall.shape[-1]
    cells = LAT * FIELDS
    up = lax.rem(t + 1, tiles)
    down = lax.rem(t + tiles - 1, tiles)
    left = lax.rem(m + windows - 1, windows)
    right = lax.rem(m + 1, windows)
    edge_low = jnp.where(t == 0, 0.0, 1.0).astype(F32)
    edge_high = jnp.where(t == tiles - 1, 0.0, 1.0).astype(F32)

    fetches = [
        pltpu.make_async_copy(source, target, raw_s.at[i])
        for i, (source, target) in enumerate(
            (
                (cell_hbm, cell_in),
                (value_hbm, value_in),
                (weight_hbm, weight_in),
                (count_hbm, count_in),
                (east_hbm, coef3.at[0]),
                (north_hbm, coef3.at[1]),
                (diff_hbm, coef3.at[2]),
                (bv_hbm, bvraw),
            )
        )
    ]
    for fetch in fetches:
        fetch.start()

    barrier = pltpu.get_barrier_semaphore()

    def greet_tile(d, token):
        pl.semaphore_signal(
            barrier, inc=1, device_id=(m, lax.rem(t + d, tiles)), device_id_type=MESH
        )
        return token

    def greet_tm(d, token):
        for where in (t, down, up):
            pl.semaphore_signal(
                barrier, inc=1, device_id=(lax.rem(m + d, windows), where), device_id_type=MESH
            )
        return token

    lax.fori_loop(1, tiles, greet_tile, 0)
    lax.fori_loop(1, windows, greet_tm, 0)

    lane = lax.broadcasted_iota(jnp.int32, (1, 128), 1)
    quarter = lane // CAP
    slot = lane - CAP * quarter
    mine = lax.rem(t, 4)

    def floor_div(value, by):
        return jnp.floor((value + 0.5) * (1.0 / by))

    for fetch in fetches[:4]:
        fetch.wait()
    for a in range(tiles // 4):
        part = slice(a * 128, (a + 1) * 128)
        cell = cell_in[0:1, part].astype(F32)
        row = floor_div(cell, LON)
        lon = cell - LON * row
        variable = floor_div(row, 2 * LAT)
        rest = row - 2 * LAT * variable
        level = floor_div(rest, LAT)
        place = FIELDS * (rest - LAT * level) + 2 * variable + level
        filled = jnp.where(
            quarter < 2,
            jnp.where(quarter == 0, count_in[0, 4 * a], count_in[0, 4 * a + 1]),
            jnp.where(quarter == 2, count_in[0, 4 * a + 2], count_in[0, 4 * a + 3]),
        )
        weight = jnp.where(slot < filled, weight_in[0:1, part], 0.0)
        block = jnp.concatenate(
            [place * LON + lon, value_in[0:1, part], weight, jnp.zeros((1, 128), F32)], axis=0
        )
        for b in range(4):
            turned = pltpu.roll(block, CAP * lax.rem(mine + 4 - b, 4), 1)
            obs0[4 * a + b] = jnp.where(quarter == mine, turned, 0.0)

    for ref in (carry, carryn, carrys):
        for sweep in range(3):
            ref[sweep * groups] = jnp.zeros(ref.shape[1:], F32)

    def cut(load, c):
        start = c * chunk - margin
        if start < 0:
            return jnp.concatenate([load(LON + start, LON), load(0, LANES + start)], axis=1)
        if start + LANES > LON:
            return jnp.concatenate([load(start, LON), load(0, start + LANES - LON)], axis=1)
        return load(start, start + LANES)

    for fetch in fetches[4:7]:
        fetch.wait()
    for r in range(LAT):
        for c in range(3):
            q = (r * 3 + c) * 2
            coef72[q // 8, q % 8 : q % 8 + 2, :] = coef3[c, :, r, :]
    for c in range(windows):
        for q in range(LAT * 6 // 8):
            coef_in[c, q] = cut(lambda a, b, q=q: coef72[q, :, a:b], c)
    craw[m] = coef_in[m]

    pl.semaphore_wait(barrier, tiles - 1 + 3 * (windows - 1))

    def remote(source, target, send, recv, where):
        return pltpu.make_async_remote_copy(
            src_ref=source,
            dst_ref=target,
            send_sem=send,
            recv_sem=recv,
            device_id=where,
            device_id_type=MESH,
        )

    def obs_copy(d):
        peer = lax.rem(t + d, tiles)
        return remote(obs0.at[peer], obs1.at[t], obs_s.at[d], obs_r.at[d], (m, peer))

    def obs_start(d, token):
        obs_copy(d).start()
        return token

    lax.fori_loop(1, tiles, obs_start, 0)


    def coef_copy(d):
        peer = lax.rem(m + d, windows)
        return remote(coef_in.at[peer], craw.at[m], c_s.at[d], c_r.at[m], (peer, t))

    def bv_copy(d):
        peer = lax.rem(m + d, windows)
        return remote(bvpack.at[peer], bvr.at[m], bv_s.at[d], bv_r.at[m], (peer, t))

    def coef_start(d, token):
        coef_copy(d).start()
        return token

    @pl.when(m >= windows - GROUP)
    def _():
        lax.fori_loop(1, windows, coef_start, 0)

    fetches[7].wait()
    for c in range(windows):
        for r in range(LAT):
            bvpack[c, r] = cut(lambda a, b, r=r: bvraw[:, r, a:b], c)

    @pl.when(m < windows - GROUP)
    def _():
        lax.fori_loop(1, windows, coef_start, 0)

    bvr[m] = bvpack[m]

    obs1[t] = obs0[t]

    def obs_wait(d, token):
        obs_copy(d).wait_recv()
        return token

    lax.fori_loop(1, tiles, obs_wait, 0)
    for j in range(tiles // 4):
        merged = obs1[4 * j] + obs1[4 * j + 1] + obs1[4 * j + 2] + obs1[4 * j + 3]
        for c in range(3):
            obsall[m, 0, c, :, j * 128 : (j + 1) * 128] = merged[c : c + 1]

    def ob2_copy(d, n):
        peer = lax.rem(m + d, windows)
        where = (t, up, down)[n]
        return remote(
            obsall.at[m, 0], obsall.at[m, n], ob2_s.at[n, d], ob2_r.at[n, m], (peer, where)
        )

    def ob2_start(d, token):
        for n in range(3):
            ob2_copy(d, n).start()
        return token

    for n in (1, 2):
        ob2_copy(0, n).start()
    lax.fori_loop(1, windows, ob2_start, 0)

    def bv_start(d, token):
        bv_copy(d).start()
        return token

    lax.fori_loop(1, windows, bv_start, 0)

    def from_peer(ref, sem, k):
        @pl.when(k != m)
        def _():
            remote(ref.at[k], ref.at[k], sem.at[k], sem.at[k], (k, t)).wait_recv()

    whole = LAT * 6 // 8
    edge_tiles = HALO * 6 // 8

    def coef_low(k, j):
        size = -(-REACH[j] * 6 // 8)
        return remote(
            craw.at[k, 0:size], craws.at[k, 0:size], ch_s.at[0, k], ch_r.at[0, k], (m, down)
        )

    def coef_high(k, j):
        size = -(-REACH[j] * 6 // 8)
        return remote(
            craw.at[k, whole - size : whole],
            crawn.at[k, edge_tiles - size : edge_tiles],
            ch_s.at[1, k],
            ch_r.at[1, k],
            (m, up),
        )

    def coef_forward(i):
        for j in range(GROUP - 1, -1, -1):
            k = windows - GROUP - GROUP * i + j
            from_peer(craw, c_r, k)
            coef_low(k, j).start()
            coef_high(k, j).start()

    even = lax.rem(lax.broadcasted_iota(jnp.int32, (FIELDS, LANES), 0), 2) == 0

    def expand(k, j):
        coef_low(k, j).wait_recv()
        coef_high(k, j).wait_recv()
        for r in range(HALO - REACH[j], HALO + LAT + REACH[j]):
            if r < HALO:
                ref, row, edge = crawn, r, edge_low
            elif r < HALO + LAT:
                ref, row, edge = craw, r - HALO, None
            else:
                ref, row, edge = craws, r - HALO - LAT, edge_high
            picked = []
            for c in range(3):
                q = (row * 3 + c) * 2
                one = ref[k, q // 8, q % 8 : q % 8 + 1, :]
                two = ref[k, q // 8, q % 8 + 1 : q % 8 + 2, :]
                picked.append(
                    jnp.where(
                        even,
                        jnp.broadcast_to(one, (FIELDS, LANES)),
                        jnp.broadcast_to(two, (FIELDS, LANES)),
                    )
                )
            half_east, half_north, kap = 0.5 * picked[0], 0.5 * picked[1], picked[2]
            made = (
                1.0 - 4.0 * kap,
                kap - half_east,
                kap + half_east,
                kap - half_north,
                kap + half_north,
            )
            for c in range(5):
                der[k, c, r] = made[c] if edge is None else made[c] * edge

    base = m * chunk - margin

    def place_and_lane(k, n):
        code = obsall[k, n, 0]
        place = floor_div(code, LON)
        rel = (code - LON * place).astype(jnp.int32) - base
        rel = jnp.where(rel >= LON, rel - LON, rel)
        return place.astype(jnp.int32), jnp.where(rel < 0, rel + LON, rel)

    def make_hot(k, n):
        place, rel = place_and_lane(k, n)
        lanes = lax.broadcasted_iota(jnp.int32, (LANES, slots), 0)
        hot[k, n] = jnp.where(lanes == rel, 1.0, 0.0).astype(BF16)

    def row_mask(k, n, first, count):
        place, rel = place_and_lane(k, n)
        rows = lax.broadcasted_iota(jnp.int32, (count * FIELDS, slots), 0) + first * FIELDS
        return rows == place

    def scatter(it, k, j, value_of):
        reach = 2 * (j + 1)
        for n, first, count, to in (
            (0, 0, LAT, HALO),
            (1, LAT - reach, reach, HALO - reach),
            (2, 0, reach, HALO + LAT),
        ):
            mask = row_mask(k, n, first, count)
            parts = [jnp.where(mask, part, 0.0).astype(BF16) for part in split3(value_of(n))]
            sums = lax.dot_general(
                jnp.concatenate(parts, axis=0),
                hot[k, n],
                (((1,), (1,)), ((), ())),
                preferred_element_type=F32,
            )
            size = count * FIELDS
            total = sums[2 * size :] + sums[size : 2 * size] + sums[:size]
            src[it, k, to : to + count] = total.reshape(count, FIELDS, LANES)

    def inc_low(k, j):
        size = HALO - 2 * j
        return remote(
            inc.at[k, 0:size], incs.at[k, 0:size], inc_s.at[0, k], inc_r.at[0, k], (m, down)
        )

    def inc_high(k, j):
        size = HALO - 2 * j
        return remote(
            inc.at[k, LAT - size : LAT],
            incn.at[k, HALO - size : HALO],
            inc_s.at[1, k],
            inc_r.at[1, k],
            (m, up),
        )

    def carry_low(e):
        return remote(
            carry.at[e, 0:HALO], carrys.at[e], car_s.at[0, e], car_r.at[0, e], (m, down)
        )

    def carry_high(e):
        return remote(
            carry.at[e, LAT - HALO : LAT], carryn.at[e], car_s.at[1, e], car_r.at[1, e], (m, up)
        )

    steps = [(a, b) for a in (0, -1, 1) for b in (0, 1, -1)][1:]

    def innov_copy(k, n):
        a, b = steps[n]
        return remote(
            innov.at[pl.ds(k, GROUP)],
            arrived.at[n, pl.ds(k, GROUP)],
            inn_s.at[n, k // GROUP],
            inn_r.at[n, k // GROUP],
            ((left, m, right)[a + 1], (down, t, up)[b + 1]),
        )

    def three(north, own, south, index, r):
        if r < HALO:
            return north[index + (r,)]
        if r < HALO + LAT:
            return own[index + (r - HALO,)]
        return south[index + (r - HALO - LAT,)]

    def adjoint_step(load, store, k, low, high):
        to_next = None
        held = None
        for r in range(low, high):
            x = load(r)
            south = der[k, 4, r] * x
            if held is not None and r - 1 >= low + 1:
                store(r - 1, held + south)
            if r < high - 1 and r > low:
                held = (
                    der[k, 0, r] * x
                    + pltpu.roll(der[k, 1, r] * x, 1, 1)
                    + pltpu.roll(der[k, 2, r] * x, LANES - 1, 1)
                    + to_next
                )
            to_next = der[k, 3, r] * x

    def forward_step(load, store, k, low, high):
        before, here = load(low), load(low + 1)
        for r in range(low + 1, high - 1):
            after = load(r + 1)
            store(
                r,
                der[k, 0, r] * here
                + der[k, 1, r] * pltpu.roll(here, LANES - 1, 1)
                + der[k, 2, r] * pltpu.roll(here, 1, 1)
                + der[k, 3, r] * after
                + der[k, 4, r] * before,
            )
            before, here = here, after

    def keep(slot):
        def store(r, value):
            work[slot, r] = value

        return store

    def wait_carry(i, e):
        @pl.when(i > 0)
        def _():
            carry_low(e).wait_recv()
            carry_high(e).wait_recv()

    def send_carry(i, e):
        @pl.when(i < groups - 1)
        def _():
            carry_low(e).start()
            carry_high(e).start()

    def adjoint_group(it, i, done):
        e = 2 * it * groups + i
        top = windows - 1 - GROUP * i
        wait_carry(i, e)
        for j in range(GROUP):
            k = top - j

            def load(r, j=j, k=k):
                if j == 0:
                    old = three(carryn, carry, carrys, (e,), r)
                else:
                    old = work[0, r]
                return old + src[it, k, r]

            low, high = 2 * j, ROWS - 2 * j
            adjoint_step(load, keep(1), k, low, high)
            adjoint_step(lambda r: work[1, r], keep(0), k, low + 1, high - 1)
            if j == GROUP - 1:

                @pl.when(i < groups - 1)
                def _():
                    carry[e + 1] = work[0, HALO : HALO + LAT]

                send_carry(i, e + 1)
            done(k)

    coef_forward(0)

    def prepare(i):
        for j in range(GROUP - 1, -1, -1):
            k = windows - GROUP - GROUP * i + j
            for n in range(3):
                sem = ob2_r.at[n, k]
                if n == 0:

                    @pl.when(k != m)
                    def _(k=k, sem=sem):
                        remote(
                            obsall.at[k, 0], obsall.at[k, 0], sem, sem, (k, t)
                        ).wait_recv()

                else:
                    remote(
                        obsall.at[k, n], obsall.at[k, n], sem, sem, (k, (down, up)[n - 1])
                    ).wait_recv()
                make_hot(k, n)
            scatter(0, k, j, lambda n, k=k: obsall[k, n, 2] * (0.0 - obsall[k, n, 1]))

    def expand_group(i):
        for j in range(GROUP - 1, -1, -1):
            expand(windows - GROUP - GROUP * i + j, j)

    prepare(0)
    for i in range(1, groups):
        coef_forward(i)
    expand_group(0)

    def increments(i):
        for j in range(GROUP):
            k = windows - GROUP - GROUP * i + j
            from_peer(bvr, bv_r, k)
            inc[k] = -0.5 * (bvr[k] * inc[k])
            inc_low(k, j).start()
            inc_high(k, j).start()

    def first(i, token):
        def done(k):
            inc[k] = work[0, HALO : HALO + LAT]

        adjoint_group(0, i, done)

        @pl.when(i < groups - 1)
        def _():
            prepare(i + 1)
            expand_group(i + 1)

        increments(i)
        return token

    lax.fori_loop(0, groups, first, 0)

    def observe(i):
        for j in range(GROUP):
            k = GROUP * i + j
            parts = split3(states[k].reshape(cells, LANES))
            picked = jnp.dot(
                jnp.concatenate([part.astype(BF16) for part in parts], axis=0),
                hot[k, 0],
                preferred_element_type=F32,
            )
            total = picked[2 * cells :] + picked[cells : 2 * cells] + picked[:cells]
            seen = jnp.sum(jnp.where(row_mask(k, 0, 0, LAT), total, 0.0), axis=0, keepdims=True)
            place, rel = place_and_lane(k, 0)
            own = (rel >= margin) & (rel < margin + chunk)
            innov[k] = jnp.where(own, obsall[k, 0, 2] * (seen - obsall[k, 0, 1]), 0.0)
        for n in range(8):
            innov_copy(GROUP * i, n).start()

    def second(i, token):
        @pl.when(i > 0)
        def _():
            observe(i - 1)

        e = groups + i
        wait_carry(i, e)
        for j in range(GROUP):
            k = GROUP * i + j
            inc_low(k, j).wait_recv()
            inc_high(k, j).wait_recv()

            def load(r, j=j, k=k):
                if j == 0:
                    old = three(carryn, carry, carrys, (e,), r)
                else:
                    old = work[0, r]
                total = old + three(incn, inc, incs, (k,), r)
                if r < HALO:
                    return total * edge_low
                if r >= HALO + LAT:
                    return total * edge_high
                return total

            low, high = 2 * j, ROWS - 2 * j
            forward_step(load, keep(1), k, low, high)
            forward_step(lambda r: work[1, r], keep(0), k, low + 1, high - 1)
            if j == GROUP - 1:

                @pl.when(i < groups - 1)
                def _():
                    carry[e + 1] = work[0, HALO : HALO + LAT]

                send_carry(i, e + 1)
            states[k] = work[0, HALO : HALO + LAT]
        return token

    lax.fori_loop(0, groups, second, 0)
    observe(groups - 1)

    def regrid(i):
        k = windows - GROUP - GROUP * i
        for n in range(8):
            innov_copy(k, n).wait_recv()

        def total(n, k):
            b = (0, 1, -1)[n]
            found = [arrived[x, k] for x in range(8) if steps[x][1] == b]
            if n == 0:
                found.append(innov[k])
            return found[0] + found[1] + found[2]

        for j in range(GROUP - 1, -1, -1):
            scatter(1, k + j, j, lambda n, k=k + j: total(n, k))

    regrid(0)

    def out_copy(k):
        return remote(final.at[k], result.at[m], out_s.at[k], out_r.at[m], (k, t))


    def third(i, token):
        def done(k):
            old = inc[k]
            states[k] = old - 0.5 * (old + bvr[k] * work[0, HALO : HALO + LAT])
            for r in range(0, LAT, 2):
                pair = []
                for e in range(2):
                    row = pltpu.roll(states[k, r + e], LANES - margin, 1)
                    final[k, r + e] = row[:, :128]
                    pair.append(row[:, 128:])
                final[k, LAT + r // 2] = jnp.where(lane < 64, pair[0], pltpu.roll(pair[1], 64, 1))

            @pl.when(k != m)
            def _():
                out_copy(k).start()

            @pl.when(k == m)
            def _():
                result[k] = final[k]

        adjoint_group(1, i, done)

        @pl.when(i < groups - 1)
        def _():
            regrid(i + 1)

        return token

    lax.fori_loop(0, groups, third, 0)

    def finish_obs(d, token):
        obs_copy(d).wait_send()
        return token

    lax.fori_loop(1, tiles, finish_obs, 0)

    def finish_tm(d, token):
        coef_copy(d).wait_send()
        bv_copy(d).wait_send()
        for n in range(3):
            ob2_copy(d, n).wait_send()
        return token

    for n in (1, 2):
        ob2_copy(0, n).wait_send()
    lax.fori_loop(1, windows, finish_tm, 0)

    def finish_groups(i, token):
        for j in range(GROUP):
            k = GROUP * i + j
            coef_low(k, j).wait_send()
            coef_high(k, j).wait_send()
            inc_low(k, j).wait_send()
            inc_high(k, j).wait_send()
        for n in range(8):
            innov_copy(GROUP * i, n).wait_send()

        @pl.when(i > 0)
        def _():
            for sweep in range(3):
                carry_low(sweep * groups + i).wait_send()
                carry_high(sweep * groups + i).wait_send()

        return token

    lax.fori_loop(0, groups, finish_groups, 0)

    def finish_windows(k, token):
        @pl.when(k != m)
        def _():
            remote(final.at[k], result.at[k], out_s.at[k], out_r.at[k], (k, t)).wait_recv()
            out_copy(k).wait_send()

        return token

    lax.fori_loop(0, windows, finish_windows, 0)
    tail = chunk - 128
    for r in range(LAT):
        first_lane = 64 * (r % 2)
        pieces = []
        for c in range(windows):
            pieces.append(result[c, r])
            pieces.append(result[c, LAT + r // 2, :, first_lane : first_lane + tail])
        out_ref[:, r, :] = jnp.concatenate(pieces, axis=1)


def per_device(
    advect_east, advect_north, diffusion, background_var, obs_cell, obs_value, obs_weight, obs_count
):
    windows = lax.axis_size("tm")
    tiles = lax.axis_size("tile")
    groups = windows // GROUP
    slots = tiles * CAP
    field = (FIELDS, LANES)
    dma = pltpu.SemaphoreType.DMA
    out = pl.pallas_call(
        functools.partial(kernel, windows, tiles),
        out_shape=jax.ShapeDtypeStruct((FIELDS, LAT, LON), F32),
        in_specs=[pl.BlockSpec(memory_space=pl.ANY)] * 8,
        out_specs=pl.BlockSpec(memory_space=pltpu.VMEM),
        scratch_shapes=[
            pltpu.VMEM((3, 2, LAT, LON), F32),
            pltpu.VMEM((LAT * 6 // 8, 8, LON), F32),
            pltpu.VMEM((windows, LAT * 6 // 8, 8, LANES), F32),
            pltpu.VMEM((1, slots), jnp.int32),
            pltpu.VMEM((1, slots), F32),
            pltpu.VMEM((1, slots), F32),
            pltpu.SMEM((1, tiles), jnp.int32),
            pltpu.VMEM((tiles, 4, 128), F32),
            pltpu.VMEM((tiles, 4, 128), F32),
            pltpu.VMEM((windows, 3, 3, 1, slots), F32),
            pltpu.VMEM((windows, LAT * 6 // 8, 8, LANES), F32),
            pltpu.VMEM((windows, HALO * 6 // 8, 8, LANES), F32),
            pltpu.VMEM((windows, HALO * 6 // 8, 8, LANES), F32),
            pltpu.VMEM((windows, 5, ROWS) + field, F32),
            pltpu.VMEM((FIELDS, LAT, LON), F32),
            pltpu.VMEM((windows, LAT) + field, F32),
            pltpu.VMEM((windows, LAT) + field, F32),
            pltpu.VMEM((windows, 3, LANES, slots), BF16),
            pltpu.VMEM((2, windows, ROWS) + field, F32),
            pltpu.VMEM((windows, LAT) + field, F32),
            pltpu.VMEM((windows, HALO) + field, F32),
            pltpu.VMEM((windows, HALO) + field, F32),
            pltpu.VMEM((windows, LAT) + field, F32),
            pltpu.VMEM((windows, LAT * 3 // 2, FIELDS, 128), F32),
            pltpu.VMEM((3 * groups, LAT) + field, F32),
            pltpu.VMEM((3 * groups, HALO) + field, F32),
            pltpu.VMEM((3 * groups, HALO) + field, F32),
            pltpu.VMEM((windows, LAT * 3 // 2, FIELDS, 128), F32),
            pltpu.VMEM((2, ROWS) + field, F32),
            pltpu.VMEM((windows, 1, slots), F32),
            pltpu.VMEM((8, windows, 1, slots), F32),
            dma((tiles,)),
            dma((tiles,)),
            dma((3, windows)),
            dma((3, windows)),
            dma((windows,)),
            dma((windows,)),
            dma((2, windows)),
            dma((2, windows)),
            dma((8,)),
            dma((windows,)),
            dma((windows,)),
            dma((2, windows)),
            dma((2, windows)),
            dma((2, 3 * groups)),
            dma((2, 3 * groups)),
            dma((8, groups)),
            dma((8, groups)),
            dma((windows,)),
            dma((windows,)),
        ],
        compiler_params=pltpu.CompilerParams(
            collective_id=0, has_side_effects=True, vmem_limit_bytes=48 * 1024 * 1024
        ),
    )(
        advect_east[0],
        advect_north[0],
        diffusion[0],
        background_var.reshape(FIELDS, LAT, LON),
        obs_cell.reshape(1, slots),
        obs_value.reshape(1, slots),
        obs_weight.reshape(1, slots),
        obs_count.reshape(1, tiles),
    )
    return out.reshape(1, FIELDS // 2, 2, LAT, LON)


def solution(mesh):
    return jax.shard_map(
        per_device,
        mesh=mesh,
        in_specs=(
            P("tm", None, "tile", None),
            P("tm", None, "tile", None),
            P("tm", None, "tile", None),
            P("tm", None, None, "tile", None),
            P("tm", "tile", None),
            P("tm", "tile", None),
            P("tm", "tile", None),
            P("tm", "tile", None),
        ),
        out_specs=P("tm", None, None, "tile", None),
        check_vma=False,
    )
```

```python
import functools

import jax
import jax.numpy as jnp
from jax import lax
from jax.experimental import pallas as pl
from jax.experimental.pallas import tpu as pltpu
from jax.sharding import PartitionSpec as P

MESH = pl.DeviceIdType.MESH
F32 = jnp.float32
BF16 = jnp.bfloat16
LON = 1440
LAT = 12
CAP = 32
FIELDS = 8
LANES = 256
GROUP = 4
HALO = 2 * GROUP
ROWS = LAT + 2 * HALO
REACH = [max(2 * (GROUP - j) - 1, 2 * (j + 1)) for j in range(GROUP)]


def split3(value):
    high = value.astype(BF16).astype(F32)
    rest = value - high
    middle = rest.astype(BF16).astype(F32)
    return high, middle, rest - middle


def kernel(
    windows,
    tiles,
    east_hbm,
    north_hbm,
    diff_hbm,
    bv_hbm,
    cell_hbm,
    value_hbm,
    weight_hbm,
    count_hbm,
    out_ref,
    coef3,
    coef72,
    coef_in,
    cell_in,
    value_in,
    weight_in,
    count_in,
    obs0,
    obs1,
    obsall,
    craw,
    crawn,
    craws,
    der,
    bvraw,
    bv8,
    bvpack,
    bvr,
    hot,
    src,
    inc,
    incn,
    incs,
    states,
    final,
    carry,
    carryn,
    carrys,
    work,
    innov,
    arrived,
    obs_s,
    obs_r,
    ob2_s,
    ob2_r,
    c_s,
    c_r,
    ch_s,
    ch_r,
    raw_s,
    bv_s,
    bv_r,
    inc_s,
    inc_r,
    car_s,
    car_r,
    inn_s,
    inn_r,
    out_s,
    out_r,
):
    m = lax.axis_index("tm")
    t = lax.axis_index("tile")
    chunk = LON // windows
    margin = (LANES - chunk) // 2
    groups = windows // GROUP
    slots = obsall.shape[-1]
    cells = LAT * FIELDS
    up = lax.rem(t + 1, tiles)
    down = lax.rem(t + tiles - 1, tiles)
    left = lax.rem(m + windows - 1, windows)
    right = lax.rem(m + 1, windows)
    edge_low = jnp.where(t == 0, 0.0, 1.0).astype(F32)
    edge_high = jnp.where(t == tiles - 1, 0.0, 1.0).astype(F32)

    fetches = [
        pltpu.make_async_copy(source, target, raw_s.at[i])
        for i, (source, target) in enumerate(
            (
                (cell_hbm, cell_in),
                (value_hbm, value_in),
                (weight_hbm, weight_in),
                (count_hbm, count_in),
                (east_hbm, coef3.at[0]),
                (north_hbm, coef3.at[1]),
                (diff_hbm, coef3.at[2]),
                (bv_hbm, bvraw),
            )
        )
    ]
    for fetch in fetches:
        fetch.start()

    barrier = pltpu.get_barrier_semaphore()

    def greet_tile(d, token):
        pl.semaphore_signal(
            barrier, inc=1, device_id=(m, lax.rem(t + d, tiles)), device_id_type=MESH
        )
        return token

    def greet_tm(d, token):
        for where in (t, down, up):
            pl.semaphore_signal(
                barrier, inc=1, device_id=(lax.rem(m + d, windows), where), device_id_type=MESH
            )
        return token

    lax.fori_loop(1, tiles, greet_tile, 0)
    lax.fori_loop(1, windows, greet_tm, 0)

    lane = lax.broadcasted_iota(jnp.int32, (1, 128), 1)
    quarter = lane // CAP
    slot = lane - CAP * quarter
    mine = lax.rem(t, 4)

    def floor_div(value, by):
        return jnp.floor((value + 0.5) * (1.0 / by))

    for fetch in fetches[:4]:
        fetch.wait()
    for a in range(tiles // 4):
        part = slice(a * 128, (a + 1) * 128)
        cell = cell_in[0:1, part].astype(F32)
        row = floor_div(cell, LON)
        lon = cell - LON * row
        variable = floor_div(row, 2 * LAT)
        rest = row - 2 * LAT * variable
        level = floor_div(rest, LAT)
        place = FIELDS * (rest - LAT * level) + 2 * variable + level
        filled = jnp.where(
            quarter < 2,
            jnp.where(quarter == 0, count_in[0, 4 * a], count_in[0, 4 * a + 1]),
            jnp.where(quarter == 2, count_in[0, 4 * a + 2], count_in[0, 4 * a + 3]),
        )
        weight = jnp.where(slot < filled, weight_in[0:1, part], 0.0)
        block = jnp.concatenate(
            [place * LON + lon, value_in[0:1, part], weight, jnp.zeros((1, 128), F32)], axis=0
        )
        for b in range(4):
            turned = pltpu.roll(block, CAP * lax.rem(mine + 4 - b, 4), 1)
            obs0[4 * a + b] = jnp.where(quarter == mine, turned, 0.0)

    for ref in (carry, carryn, carrys):
        for sweep in range(3):
            ref[sweep * groups] = jnp.zeros(ref.shape[1:], F32)

    def cut(load, c):
        start = c * chunk - margin
        if start < 0:
            return jnp.concatenate([load(LON + start, LON), load(0, LANES + start)], axis=1)
        if start + LANES > LON:
            return jnp.concatenate([load(start, LON), load(0, start + LANES - LON)], axis=1)
        return load(start, start + LANES)

    for fetch in fetches[4:7]:
        fetch.wait()
    for r in range(LAT):
        for c in range(3):
            q = (r * 3 + c) * 2
            coef72[q // 8, q % 8 : q % 8 + 2, :] = coef3[c, r]
    for c in range(windows):
        for q in range(LAT * 6 // 8):
            coef_in[c, q] = cut(lambda a, b, q=q: coef72[q, :, a:b], c)
    craw[m] = coef_in[m]

    pl.semaphore_wait(barrier, tiles - 1 + 3 * (windows - 1))

    def remote(source, target, send, recv, where):
        return pltpu.make_async_remote_copy(
            src_ref=source,
            dst_ref=target,
            send_sem=send,
            recv_sem=recv,
            device_id=where,
            device_id_type=MESH,
        )

    def obs_copy(d):
        peer = lax.rem(t + d, tiles)
        return remote(obs0.at[peer], obs1.at[t], obs_s.at[d], obs_r.at[d], (m, peer))

    def obs_start(d, token):
        obs_copy(d).start()
        return token

    lax.fori_loop(1, tiles, obs_start, 0)


    def coef_copy(d):
        peer = lax.rem(m + d, windows)
        return remote(coef_in.at[peer], craw.at[m], c_s.at[d], c_r.at[m], (peer, t))

    def bv_copy(d):
        peer = lax.rem(m + d, windows)
        return remote(bvpack.at[peer], bvr.at[m], bv_s.at[d], bv_r.at[m], (peer, t))

    def coef_start(d, token):
        coef_copy(d).start()
        return token

    @pl.when(m >= windows - GROUP)
    def _():
        lax.fori_loop(1, windows, coef_start, 0)

    fetches[7].wait()
    for r in range(LAT):
        for v in range(FIELDS // 2):
            bv8[r, 2 * v : 2 * v + 2, :] = bvraw[v, r]
    for c in range(windows):
        for r in range(LAT):
            bvpack[c, r] = cut(lambda a, b, r=r: bv8[r, :, a:b], c)

    @pl.when(m < windows - GROUP)
    def _():
        lax.fori_loop(1, windows, coef_start, 0)

    bvr[m] = bvpack[m]

    obs1[t] = obs0[t]

    def obs_wait(d, token):
        obs_copy(d).wait_recv()
        return token

    lax.fori_loop(1, tiles, obs_wait, 0)
    for j in range(tiles // 4):
        merged = obs1[4 * j] + obs1[4 * j + 1] + obs1[4 * j + 2] + obs1[4 * j + 3]
        for c in range(3):
            obsall[m, 0, c, :, j * 128 : (j + 1) * 128] = merged[c : c + 1]

    def ob2_copy(d, n):
        peer = lax.rem(m + d, windows)
        where = (t, up, down)[n]
        return remote(
            obsall.at[m, 0], obsall.at[m, n], ob2_s.at[n, d], ob2_r.at[n, m], (peer, where)
        )

    def ob2_start(d, token):
        for n in range(3):
            ob2_copy(d, n).start()
        return token

    for n in (1, 2):
        ob2_copy(0, n).start()
    lax.fori_loop(1, windows, ob2_start, 0)

    def bv_start(d, token):
        bv_copy(d).start()
        return token

    lax.fori_loop(1, windows, bv_start, 0)

    def from_peer(ref, sem, k):
        @pl.when(k != m)
        def _():
            remote(ref.at[k], ref.at[k], sem.at[k], sem.at[k], (k, t)).wait_recv()

    whole = LAT * 6 // 8
    edge_tiles = HALO * 6 // 8

    def coef_low(k, j):
        size = -(-REACH[j] * 6 // 8)
        return remote(
            craw.at[k, 0:size], craws.at[k, 0:size], ch_s.at[0, k], ch_r.at[0, k], (m, down)
        )

    def coef_high(k, j):
        size = -(-REACH[j] * 6 // 8)
        return remote(
            craw.at[k, whole - size : whole],
            crawn.at[k, edge_tiles - size : edge_tiles],
            ch_s.at[1, k],
            ch_r.at[1, k],
            (m, up),
        )

    def coef_forward(i):
        for j in range(GROUP - 1, -1, -1):
            k = windows - GROUP - GROUP * i + j
            from_peer(craw, c_r, k)
            coef_low(k, j).start()
            coef_high(k, j).start()

    even = lax.rem(lax.broadcasted_iota(jnp.int32, (FIELDS, LANES), 0), 2) == 0

    def expand(k, j):
        coef_low(k, j).wait_recv()
        coef_high(k, j).wait_recv()
        for r in range(HALO - REACH[j], HALO + LAT + REACH[j]):
            if r < HALO:
                ref, row, edge = crawn, r, edge_low
            elif r < HALO + LAT:
                ref, row, edge = craw, r - HALO, None
            else:
                ref, row, edge = craws, r - HALO - LAT, edge_high
            picked = []
            for c in range(3):
                q = (row * 3 + c) * 2
                one = ref[k, q // 8, q % 8 : q % 8 + 1, :]
                two = ref[k, q // 8, q % 8 + 1 : q % 8 + 2, :]
                picked.append(
                    jnp.where(
                        even,
                        jnp.broadcast_to(one, (FIELDS, LANES)),
                        jnp.broadcast_to(two, (FIELDS, LANES)),
                    )
                )
            half_east, half_north, kap = 0.5 * picked[0], 0.5 * picked[1], picked[2]
            made = (
                1.0 - 4.0 * kap,
                kap - half_east,
                kap + half_east,
                kap - half_north,
                kap + half_north,
            )
            for c in range(5):
                der[k, c, r] = made[c] if edge is None else made[c] * edge

    base = m * chunk - margin

    def place_and_lane(k, n):
        code = obsall[k, n, 0]
        place = floor_div(code, LON)
        rel = (code - LON * place).astype(jnp.int32) - base
        rel = jnp.where(rel >= LON, rel - LON, rel)
        return place.astype(jnp.int32), jnp.where(rel < 0, rel + LON, rel)

    def make_hot(k, n):
        place, rel = place_and_lane(k, n)
        lanes = lax.broadcasted_iota(jnp.int32, (LANES, slots), 0)
        hot[k, n] = jnp.where(lanes == rel, 1.0, 0.0).astype(BF16)

    def row_mask(k, n, first, count):
        place, rel = place_and_lane(k, n)
        rows = lax.broadcasted_iota(jnp.int32, (count * FIELDS, slots), 0) + first * FIELDS
        return rows == place

    def scatter(it, k, j, value_of):
        reach = 2 * (j + 1)
        for n, first, count, to in (
            (0, 0, LAT, HALO),
            (1, LAT - reach, reach, HALO - reach),
            (2, 0, reach, HALO + LAT),
        ):
            mask = row_mask(k, n, first, count)
            parts = [jnp.where(mask, part, 0.0).astype(BF16) for part in split3(value_of(n))]
            sums = lax.dot_general(
                jnp.concatenate(parts, axis=0),
                hot[k, n],
                (((1,), (1,)), ((), ())),
                preferred_element_type=F32,
            )
            size = count * FIELDS
            total = sums[2 * size :] + sums[size : 2 * size] + sums[:size]
            src[it, k, to : to + count] = total.reshape(count, FIELDS, LANES)

    def inc_low(k, j):
        size = HALO - 2 * j
        return remote(
            inc.at[k, 0:size], incs.at[k, 0:size], inc_s.at[0, k], inc_r.at[0, k], (m, down)
        )

    def inc_high(k, j):
        size = HALO - 2 * j
        return remote(
            inc.at[k, LAT - size : LAT],
            incn.at[k, HALO - size : HALO],
            inc_s.at[1, k],
            inc_r.at[1, k],
            (m, up),
        )

    def carry_low(e):
        return remote(
            carry.at[e, 0:HALO], carrys.at[e], car_s.at[0, e], car_r.at[0, e], (m, down)
        )

    def carry_high(e):
        return remote(
            carry.at[e, LAT - HALO : LAT], carryn.at[e], car_s.at[1, e], car_r.at[1, e], (m, up)
        )

    steps = [(a, b) for a in (0, -1, 1) for b in (0, 1, -1)][1:]

    def innov_copy(k, n):
        a, b = steps[n]
        return remote(
            innov.at[pl.ds(k, GROUP)],
            arrived.at[n, pl.ds(k, GROUP)],
            inn_s.at[n, k // GROUP],
            inn_r.at[n, k // GROUP],
            ((left, m, right)[a + 1], (down, t, up)[b + 1]),
        )

    def three(north, own, south, index, r):
        if r < HALO:
            return north[index + (r,)]
        if r < HALO + LAT:
            return own[index + (r - HALO,)]
        return south[index + (r - HALO - LAT,)]

    def adjoint_step(load, store, k, low, high):
        to_next = None
        held = None
        for r in range(low, high):
            x = load(r)
            south = der[k, 4, r] * x
            if held is not None and r - 1 >= low + 1:
                store(r - 1, held + south)
            if r < high - 1 and r > low:
                held = (
                    der[k, 0, r] * x
                    + pltpu.roll(der[k, 1, r] * x, 1, 1)
                    + pltpu.roll(der[k, 2, r] * x, LANES - 1, 1)
                    + to_next
                )
            to_next = der[k, 3, r] * x

    def forward_step(load, store, k, low, high):
        before, here = load(low), load(low + 1)
        for r in range(low + 1, high - 1):
            after = load(r + 1)
            store(
                r,
                der[k, 0, r] * here
                + der[k, 1, r] * pltpu.roll(here, LANES - 1, 1)
                + der[k, 2, r] * pltpu.roll(here, 1, 1)
                + der[k, 3, r] * after
                + der[k, 4, r] * before,
            )
            before, here = here, after

    def keep(slot):
        def store(r, value):
            work[slot, r] = value

        return store

    def wait_carry(i, e):
        @pl.when(i > 0)
        def _():
            carry_low(e).wait_recv()
            carry_high(e).wait_recv()

    def send_carry(i, e):
        @pl.when(i < groups - 1)
        def _():
            carry_low(e).start()
            carry_high(e).start()

    def adjoint_group(it, i, done):
        e = 2 * it * groups + i
        top = windows - 1 - GROUP * i
        wait_carry(i, e)
        for j in range(GROUP):
            k = top - j

            def load(r, j=j, k=k):
                if j == 0:
                    old = three(carryn, carry, carrys, (e,), r)
                else:
                    old = work[0, r]
                return old + src[it, k, r]

            low, high = 2 * j, ROWS - 2 * j
            adjoint_step(load, keep(1), k, low, high)
            adjoint_step(lambda r: work[1, r], keep(0), k, low + 1, high - 1)
            if j == GROUP - 1:

                @pl.when(i < groups - 1)
                def _():
                    carry[e + 1] = work[0, HALO : HALO + LAT]

                send_carry(i, e + 1)
            done(k)

    coef_forward(0)

    def prepare(i):
        for j in range(GROUP - 1, -1, -1):
            k = windows - GROUP - GROUP * i + j
            for n in range(3):
                sem = ob2_r.at[n, k]
                if n == 0:

                    @pl.when(k != m)
                    def _(k=k, sem=sem):
                        remote(
                            obsall.at[k, 0], obsall.at[k, 0], sem, sem, (k, t)
                        ).wait_recv()

                else:
                    remote(
                        obsall.at[k, n], obsall.at[k, n], sem, sem, (k, (down, up)[n - 1])
                    ).wait_recv()
                make_hot(k, n)
            scatter(0, k, j, lambda n, k=k: obsall[k, n, 2] * (0.0 - obsall[k, n, 1]))

    def expand_group(i):
        for j in range(GROUP - 1, -1, -1):
            expand(windows - GROUP - GROUP * i + j, j)

    prepare(0)
    for i in range(1, groups):
        coef_forward(i)
    expand_group(0)

    def increments(i):
        for j in range(GROUP):
            k = windows - GROUP - GROUP * i + j
            from_peer(bvr, bv_r, k)
            inc[k] = -0.5 * (bvr[k] * inc[k])
            inc_low(k, j).start()
            inc_high(k, j).start()

    def first(i, token):
        def done(k):
            inc[k] = work[0, HALO : HALO + LAT]

        adjoint_group(0, i, done)

        @pl.when(i < groups - 1)
        def _():
            prepare(i + 1)
            expand_group(i + 1)

        increments(i)
        return token

    lax.fori_loop(0, groups, first, 0)

    def observe(i):
        for j in range(GROUP):
            k = GROUP * i + j
            parts = split3(states[k].reshape(cells, LANES))
            picked = jnp.dot(
                jnp.concatenate([part.astype(BF16) for part in parts], axis=0),
                hot[k, 0],
                preferred_element_type=F32,
            )
            total = picked[2 * cells :] + picked[cells : 2 * cells] + picked[:cells]
            seen = jnp.sum(jnp.where(row_mask(k, 0, 0, LAT), total, 0.0), axis=0, keepdims=True)
            place, rel = place_and_lane(k, 0)
            own = (rel >= margin) & (rel < margin + chunk)
            innov[k] = jnp.where(own, obsall[k, 0, 2] * (seen - obsall[k, 0, 1]), 0.0)
        for n in range(8):
            innov_copy(GROUP * i, n).start()

    def second(i, token):
        @pl.when(i > 0)
        def _():
            observe(i - 1)

        e = groups + i
        wait_carry(i, e)
        for j in range(GROUP):
            k = GROUP * i + j
            inc_low(k, j).wait_recv()
            inc_high(k, j).wait_recv()

            def load(r, j=j, k=k):
                if j == 0:
                    old = three(carryn, carry, carrys, (e,), r)
                else:
                    old = work[0, r]
                total = old + three(incn, inc, incs, (k,), r)
                if r < HALO:
                    return total * edge_low
                if r >= HALO + LAT:
                    return total * edge_high
                return total

            low, high = 2 * j, ROWS - 2 * j
            forward_step(load, keep(1), k, low, high)
            forward_step(lambda r: work[1, r], keep(0), k, low + 1, high - 1)
            if j == GROUP - 1:

                @pl.when(i < groups - 1)
                def _():
                    carry[e + 1] = work[0, HALO : HALO + LAT]

                send_carry(i, e + 1)
            states[k] = work[0, HALO : HALO + LAT]
        return token

    lax.fori_loop(0, groups, second, 0)
    observe(groups - 1)

    def regrid(i):
        k = windows - GROUP - GROUP * i
        for n in range(8):
            innov_copy(k, n).wait_recv()

        def total(n, k):
            b = (0, 1, -1)[n]
            found = [arrived[x, k] for x in range(8) if steps[x][1] == b]
            if n == 0:
                found.append(innov[k])
            return found[0] + found[1] + found[2]

        for j in range(GROUP - 1, -1, -1):
            scatter(1, k + j, j, lambda n, k=k + j: total(n, k))

    regrid(0)

    def out_copy(k):
        return remote(final.at[k], out_ref.at[m], out_s.at[k], out_r.at[m], (k, t))


    def out_own(k):
        return pltpu.make_async_copy(final.at[k], out_ref.at[m], out_r.at[k])

    def third(i, token):
        def done(k):
            old = inc[k]
            states[k] = old - 0.5 * (old + bvr[k] * work[0, HALO : HALO + LAT])
            for r in range(0, LAT, 2):
                pair = []
                for e in range(2):
                    row = pltpu.roll(states[k, r + e], LANES - margin, 1)
                    final[k, r + e] = row[:, :128]
                    pair.append(row[:, 128:])
                final[k, LAT + r // 2] = jnp.where(lane < 64, pair[0], pltpu.roll(pair[1], 64, 1))

            @pl.when(k != m)
            def _():
                out_copy(k).start()

            @pl.when(k == m)
            def _():
                out_own(k).start()

        adjoint_group(1, i, done)

        @pl.when(i < groups - 1)
        def _():
            regrid(i + 1)

        return token

    lax.fori_loop(0, groups, third, 0)

    def finish_obs(d, token):
        obs_copy(d).wait_send()
        return token

    lax.fori_loop(1, tiles, finish_obs, 0)

    def finish_tm(d, token):
        coef_copy(d).wait_send()
        bv_copy(d).wait_send()
        for n in range(3):
            ob2_copy(d, n).wait_send()
        return token

    for n in (1, 2):
        ob2_copy(0, n).wait_send()
    lax.fori_loop(1, windows, finish_tm, 0)

    def finish_groups(i, token):
        for j in range(GROUP):
            k = GROUP * i + j
            coef_low(k, j).wait_send()
            coef_high(k, j).wait_send()
            inc_low(k, j).wait_send()
            inc_high(k, j).wait_send()
        for n in range(8):
            innov_copy(GROUP * i, n).wait_send()

        @pl.when(i > 0)
        def _():
            for sweep in range(3):
                carry_low(sweep * groups + i).wait_send()
                carry_high(sweep * groups + i).wait_send()

        return token

    lax.fori_loop(0, groups, finish_groups, 0)

    def finish_windows(k, token):
        @pl.when(k != m)
        def _():
            remote(final.at[k], out_ref.at[k], out_s.at[k], out_r.at[k], (k, t)).wait_recv()
            out_copy(k).wait_send()

        @pl.when(k == m)
        def _():
            out_own(k).wait()

        return token

    lax.fori_loop(0, windows, finish_windows, 0)


def unpack(main_ref, tail_ref, out_ref):
    windows = main_ref.shape[0]
    tail = LON // windows - 128
    for e in range(2):
        pieces = []
        for c in range(windows):
            pieces.append(main_ref[c, e])
            pieces.append(tail_ref[c, 0, :, 64 * e : 64 * e + tail])
        row = jnp.concatenate(pieces, axis=1)
        for v in range(FIELDS // 2):
            out_ref[v, e] = row[2 * v : 2 * v + 2, :]


def per_device(
    advect_east, advect_north, diffusion, background_var, obs_cell, obs_value, obs_weight, obs_count
):
    windows = lax.axis_size("tm")
    tiles = lax.axis_size("tile")
    groups = windows // GROUP
    slots = tiles * CAP
    field = (FIELDS, LANES)
    dma = pltpu.SemaphoreType.DMA
    packed = pl.pallas_call(
        functools.partial(kernel, windows, tiles),
        out_shape=jax.ShapeDtypeStruct((windows, LAT * 3 // 2, FIELDS, 128), F32),
        in_specs=[pl.BlockSpec(memory_space=pltpu.HBM)] * 8,
        out_specs=pl.BlockSpec(memory_space=pl.ANY),
        scratch_shapes=[
            pltpu.VMEM((3, LAT, 2, LON), F32),
            pltpu.VMEM((LAT * 6 // 8, 8, LON), F32),
            pltpu.VMEM((windows, LAT * 6 // 8, 8, LANES), F32),
            pltpu.VMEM((1, slots), jnp.int32),
            pltpu.VMEM((1, slots), F32),
            pltpu.VMEM((1, slots), F32),
            pltpu.SMEM((1, tiles), jnp.int32),
            pltpu.VMEM((tiles, 4, 128), F32),
            pltpu.VMEM((tiles, 4, 128), F32),
            pltpu.VMEM((windows, 3, 3, 1, slots), F32),
            pltpu.VMEM((windows, LAT * 6 // 8, 8, LANES), F32),
            pltpu.VMEM((windows, HALO * 6 // 8, 8, LANES), F32),
            pltpu.VMEM((windows, HALO * 6 // 8, 8, LANES), F32),
            pltpu.VMEM((windows, 5, ROWS) + field, F32),
            pltpu.VMEM((FIELDS // 2, LAT, 2, LON), F32),
            pltpu.VMEM((LAT, FIELDS, LON), F32),
            pltpu.VMEM((windows, LAT) + field, F32),
            pltpu.VMEM((windows, LAT) + field, F32),
            pltpu.VMEM((windows, 3, LANES, slots), BF16),
            pltpu.VMEM((2, windows, ROWS) + field, F32),
            pltpu.VMEM((windows, LAT) + field, F32),
            pltpu.VMEM((windows, HALO) + field, F32),
            pltpu.VMEM((windows, HALO) + field, F32),
            pltpu.VMEM((windows, LAT) + field, F32),
            pltpu.VMEM((windows, LAT * 3 // 2, FIELDS, 128), F32),
            pltpu.VMEM((3 * groups, LAT) + field, F32),
            pltpu.VMEM((3 * groups, HALO) + field, F32),
            pltpu.VMEM((3 * groups, HALO) + field, F32),
            pltpu.VMEM((2, ROWS) + field, F32),
            pltpu.VMEM((windows, 1, slots), F32),
            pltpu.VMEM((8, windows, 1, slots), F32),
            dma((tiles,)),
            dma((tiles,)),
            dma((3, windows)),
            dma((3, windows)),
            dma((windows,)),
            dma((windows,)),
            dma((2, windows)),
            dma((2, windows)),
            dma((8,)),
            dma((windows,)),
            dma((windows,)),
            dma((2, windows)),
            dma((2, windows)),
            dma((2, 3 * groups)),
            dma((2, 3 * groups)),
            dma((8, groups)),
            dma((8, groups)),
            dma((windows,)),
            dma((windows,)),
        ],
        compiler_params=pltpu.CompilerParams(
            collective_id=0, has_side_effects=True, vmem_limit_bytes=65000000
        ),
    )(
        advect_east[0].transpose(1, 0, 2),
        advect_north[0].transpose(1, 0, 2),
        diffusion[0].transpose(1, 0, 2),
        background_var[0].transpose(0, 2, 1, 3),
        obs_cell.reshape(1, slots),
        obs_value.reshape(1, slots),
        obs_weight.reshape(1, slots),
        obs_count.reshape(1, tiles),
    )
    out = pl.pallas_call(
        unpack,
        out_shape=jax.ShapeDtypeStruct((FIELDS // 2, LAT, 2, LON), F32),
        grid=(LAT // 2,),
        in_specs=[
            pl.BlockSpec((windows, 2, FIELDS, 128), lambda p: (0, p, 0, 0)),
            pl.BlockSpec((windows, 1, FIELDS, 128), lambda p: (0, LAT + p, 0, 0)),
        ],
        out_specs=pl.BlockSpec((FIELDS // 2, 2, 2, LON), lambda p: (0, p, 0, 0)),
    )(packed, packed)
    return out.transpose(0, 2, 1, 3)[None]


def solution(mesh):
    return jax.shard_map(
        per_device,
        mesh=mesh,
        in_specs=(
            P("tm", None, "tile", None),
            P("tm", None, "tile", None),
            P("tm", None, "tile", None),
            P("tm", None, None, "tile", None),
            P("tm", "tile", None),
            P("tm", "tile", None),
            P("tm", "tile", None),
            P("tm", "tile", None),
        ),
        out_specs=P("tm", None, None, "tile", None),
        check_vma=False,
    )
```
